512 devices in a mesh: grp: 16 (over z), seq: 32 (over x, y, core).
Axes of the slice: x: 4, y: 4, z: 16, core: 2. Of those that a mesh axis runs over, the one named last changes fastest.
Arguments:
- queries: bfloat16 [16, 8192, 2048], P('grp', 'seq'), may hold values from -24 to 24
- grad_out: bfloat16 [16, 8192, 2048], P('grp', 'seq'), may hold values from -6 to 6
- neighbour_keys: bfloat16 [16, 32, 128, 2048], P('grp', 'seq'), may hold values from -6 to 6
- neighbour_values: bfloat16 [16, 32, 128, 2048], P('grp', 'seq'), may hold values from -6 to 6
- neighbours: int32 [16, 128, 4], P('grp', 'seq'), may hold values from 0 to 15, all different within a row; in each aligned block of 4 rows (0 to 3, 4 to 7, ..., all dimensions but the last counted through in order) no two rows name the same one
Outputs:
- grad_windows: bfloat16 [16, 128, 64, 2048], P('grp', 'seq')
- grad_keys: bfloat16 [16, 32, 128, 2048], P('grp', 'seq')
- grad_values: bfloat16 [16, 32, 128, 2048], P('grp', 'seq')
The draws below stay inside these ranges and needn't reach their ends.
Inputs may be any that keep to these rules, and one draw needn't show every extreme that they name: `neighbours`: the 4 groups of a span differ; among the 4 spans of one device no group is named more than 1 times, and that many is reached.
All inputs are finite; a program needn't handle non-finite values.
Results may differ from the reference program's by a relative error of at most 0.015.
The reference program's roundings to bfloat16 on the way count: a program that leaves them out, or rounds other values in their place, can miss the bound.
Values may be sent and summed in bfloat16 or wider, within the bound.
A program may use at most 64 MiB of HBM per device.

```python
import math
import jax
import jax.numpy as jnp
import numpy as np
from jax import lax

HEAD = 128
HEADS = 16
SPAN = 64
NBR_LEN = 128
NBRS = 4
HD = 2048
CH = 4
SEQS = 16
OWNERS = 16
COLUMNS = 32
LENGTH = 8192
SPANS_SEQ = 128
CAP = 1


def draw_queries(key, part):
    base = jax.random.fold_in(key, 11)
    shape = (SEQS, LENGTH, HD)
    values = jax.random.truncated_normal(base, -6.0, 6.0, shape, jnp.float32)
    return values.astype(jnp.bfloat16)


def draw_neighbour_keys(key, part):
    base = jax.random.fold_in(key, 21)
    shape = (OWNERS, COLUMNS, NBR_LEN, HD)
    values = jax.random.truncated_normal(base, -6.0, 6.0, shape, jnp.float32)
    return values.astype(jnp.bfloat16)


def levels(own_key, shape, split, smallest, largest):
    def one(dim, blocks):
        draws = jax.random.uniform(jax.random.fold_in(jax.random.fold_in(own_key, 6), dim), (blocks,), jnp.float32, smallest / len(split), largest / len(split))
        return jnp.repeat(jnp.exp(draws), shape[dim] // blocks).reshape((-1,) + (1,) * (len(shape) - dim - 1))

    factor_of = one(*split[0])
    for cut in split[1:]:
        factor_of = factor_of * one(*cut)
    return factor_of


def shared_out(key, own, number, rows, number_of, top, reach, skew):
    ranking = jax.random.permutation(key, number_of)
    heavy_load, common = shares(number_of, rows * top, reach, skew, True), shares(number_of, rows * top, reach, skew, False)
    places = jnp.arange(number_of)

    def named(lengths, rotation):
        used = int((lengths > 0).sum())
        fixed = max(1, used // 4)
        shifted = fixed + (places - fixed + rotation * (used - fixed)) % max(1, number_of - fixed)
        return jnp.zeros((number_of,), jnp.int32).at[ranking[jnp.where(places < fixed, places, shifted)]].set(jnp.asarray(lengths, jnp.int32))

    lengths = jnp.where(number % 4 == 0, named(heavy_load, number // 4), named(common, number - number // 4 - 1))
    mixed = jax.random.permutation(jax.random.fold_in(own, 3), number_of)
    source_of, receiver = mixed[0:number_of // 2 * 2:2], mixed[1:number_of // 2 * 2:2]
    room = jnp.minimum(lengths[source_of] - 1, reach - lengths[receiver]) // 2
    room = jnp.where((source_of == ranking[0]) | (receiver == ranking[0]) | (lengths[receiver] == 0), 0, jnp.maximum(room, 0))
    shifted = jax.random.randint(jax.random.fold_in(own, 4), (number_of // 2,), 0, 1 << 20) % (room + 1)
    lengths = lengths.at[source_of].add(-shifted).at[receiver].add(shifted)
    items = jnp.searchsorted(jnp.cumsum(lengths), jnp.arange(rows * top), side="right").astype(jnp.int32)
    table = items.reshape(top, rows).T
    table = table[jax.random.permutation(jax.random.fold_in(own, 1), rows)]
    rotation = jax.random.randint(jax.random.fold_in(own, 2), (rows, 1), 0, top)
    return jnp.take_along_axis(table, (jnp.arange(top)[None, :] + rotation) % top, axis=1)


def shares(count, total, bound, lean, full):
    weights = [(1 << 20) // math.isqrt(rank ** lean) + 1 for rank in range(1, count + 1)]
    largest = bound if full else min(bound, max(-(-total // count), total * weights[0] // sum(weights)))
    least = 1 if total - largest >= count - 1 else 0
    given, surplus = [largest] + [least] * (count - 1), total - largest - least * (count - 1)
    while surplus > 0:
        movable = [i for i in range(1, count) if given[i] < largest] or [i for i in range(1, count) if given[i] < bound]
        mass, left = sum([weights[i] for i in movable]), surplus
        for i in movable:
            extra = min(bound - given[i], max(1, left * weights[i] // mass), surplus)
            given[i] = given[i] + extra
            surplus = surplus - extra
    return np.array(given)


def bell_draw(stream_key, shape, deviation, reach, split=(), kind=jnp.bfloat16):
    gain = levels(stream_key, shape, split, -0.22, 0.18) if split else 1.0
    entries = jax.random.normal(stream_key, shape, jnp.float32) * deviation * gain
    return jnp.minimum(jnp.maximum(entries, -reach), reach).astype(kind)


def setup_inputs(seed: int = 0) -> dict:
    key_of = jax.random.split(jax.random.key(seed), 6)
    queries = draw_queries(jax.random.fold_in(key_of[5], 71), 0)
    grad_out = bell_draw(key_of[1], (SEQS, LENGTH, HD), 1.0, 6.0, ((0, 16), (1, 32)))
    neighbour_keys = draw_neighbour_keys(jax.random.fold_in(key_of[5], 71), 0)
    neighbour_values = bell_draw(key_of[3], (OWNERS, COLUMNS, NBR_LEN, HD), 1.0, 6.0, ((0, 16), (1, 32)))
    neighbours_keys = jax.random.split(jax.random.fold_in(key_of[4], 1), SEQS * SPANS_SEQ // CH)
    neighbours_turns = jax.random.permutation(jax.random.fold_in(key_of[4], 3), SEQS * SPANS_SEQ // CH)
    neighbours = jax.vmap(lambda own, number: shared_out(jax.random.fold_in(key_of[4], 2), own, number, CH, OWNERS, NBRS, CAP, 2))(neighbours_keys, neighbours_turns).reshape((SEQS, SPANS_SEQ, NBRS))
    return dict(queries=queries, grad_out=grad_out, neighbour_keys=neighbour_keys, neighbour_values=neighbour_values, neighbours=neighbours)


def rounded(values):
    return lax.optimization_barrier(values.astype(jnp.bfloat16)).astype(jnp.float32)


def column(operands):
    win_query, win_grad, group_ids, col_keys, col_values = operands
    score_scale = HEAD ** -0.5
    query_f = win_query.astype(jnp.float32)
    grad_f = win_grad.astype(jnp.float32)
    key_pairs = col_keys[group_ids].astype(jnp.float32)
    value_pairs = col_values[group_ids].astype(jnp.float32)
    scores = jnp.einsum("gcqhd,gcjkhd->gcjqhk", query_f, key_pairs) * score_scale
    row_max = jnp.max(scores, axis=-1)
    exp_scores = jnp.exp(scores - row_max[..., None])
    row_total = jnp.sum(exp_scores, axis=-1)
    partial_value = jnp.einsum("gcjqhk,gcjkhd->gcjqhd", rounded(exp_scores), value_pairs) / row_total[..., None]
    dotted = jnp.sum(grad_f[:, :, None] * partial_value, axis=-1)
    top_max = jnp.max(row_max, axis=2, keepdims=True)
    weights = row_total * jnp.exp(row_max - top_max)
    weight_sum = jnp.sum(weights, axis=2)
    log_total = top_max[:, :, 0] + jnp.log(weight_sum)
    delta_rows = jnp.sum(weights * dotted, axis=2) / weight_sum
    probabilities = jnp.exp(scores - log_total[:, :, None, :, :, None])
    grad_probs = jnp.einsum("gcqhd,gcjkhd->gcjqhk", grad_f, value_pairs)
    grad_scores = rounded(probabilities * (grad_probs - delta_rows[:, :, None, :, :, None]))
    grad_query = rounded(jnp.einsum("gcjqhk,gcjkhd->gcjqhd", grad_scores, key_pairs) * score_scale)
    grad_window = jnp.sum(grad_query, axis=2).astype(jnp.bfloat16)
    value_terms = jnp.einsum("gcjqhk,gcqhd->gcjkhd", rounded(probabilities), grad_f)
    key_terms = jnp.einsum("gcjqhk,gcqhd->gcjkhd", grad_scores, query_f)
    owner_list = group_ids.reshape(-1).astype(jnp.int32)
    grad_vals = jax.ops.segment_sum(value_terms.reshape((-1,) + value_terms.shape[3:]), owner_list, num_segments=OWNERS)
    grad_keys = jax.ops.segment_sum(key_terms.reshape((-1,) + key_terms.shape[3:]), owner_list, num_segments=OWNERS) * score_scale
    return grad_window, grad_keys.astype(jnp.bfloat16), grad_vals.astype(jnp.bfloat16)


def windows(source):
    tail = jnp.zeros((SEQS, SPAN - 1, HD), source.dtype)
    shaped = jnp.concatenate([source[:, SPAN - 1:], tail], axis=1).reshape(SEQS, COLUMNS, CH, SPAN, HEADS, HEAD)
    return jnp.moveaxis(shaped, 1, 0)


def reference(queries, grad_out, neighbour_keys, neighbour_values, neighbours):
    win_query = windows(queries)
    win_grad = windows(grad_out)
    group_ids = jnp.moveaxis(neighbours.reshape(SEQS, COLUMNS, CH, NBRS), 1, 0).astype(jnp.int32)
    col_keys = jnp.moveaxis(neighbour_keys, 1, 0).reshape(COLUMNS, OWNERS, NBR_LEN, HEADS, HEAD)
    col_values = jnp.moveaxis(neighbour_values, 1, 0).reshape(COLUMNS, OWNERS, NBR_LEN, HEADS, HEAD)
    grad_win, grad_keys, grad_vals = lax.map(column, (win_query, win_grad, group_ids, col_keys, col_values))
    grad_windows = jnp.moveaxis(grad_win, 0, 1).reshape(SEQS, SPANS_SEQ, SPAN, HD)
    grad_keys = jnp.moveaxis(grad_keys, 0, 1).reshape(OWNERS, COLUMNS, NBR_LEN, HD)
    grad_values = jnp.moveaxis(grad_vals, 0, 1).reshape(OWNERS, COLUMNS, NBR_LEN, HD)
    return (grad_windows, grad_keys, grad_values)
```

```python
import jax
import jax.numpy as jnp
from jax import lax
from jax.sharding import PartitionSpec as P

HEAD = 128
SPAN = 64
NBRS = 4
CHUNKS = 4


def from_behind(array, axis, by):
    length = lax.axis_size(axis)
    pairs = [(i, i + by) for i in range(length) if 0 <= i + by < length]
    return lax.ppermute(array, axis, pairs)


def split_heads(block_rows):
    return block_rows.reshape(block_rows.shape[:-1] + (block_rows.shape[-1] // HEAD, HEAD))


def slot_forward(query_block, grad_block, key_heads, value_heads):
    query_heads = split_heads(query_block)
    scores = jnp.einsum(
        "nqhd,nkhd->nqhk", query_heads, key_heads, preferred_element_type=jnp.float32
    ) * HEAD ** (-0.5)
    row_max = jnp.max(scores, axis=-1)
    exp_scores = jnp.exp(scores - row_max[..., None])
    row_total = jnp.sum(exp_scores, axis=-1)
    partial_value = (
        jnp.einsum(
            "nqhk,nkhd->nqhd",
            exp_scores.astype(jnp.bfloat16),
            value_heads,
            preferred_element_type=jnp.float32,
        )
        / row_total[..., None]
    )
    dotted = jnp.sum(split_heads(grad_block).astype(jnp.float32) * partial_value, axis=-1)
    return (row_max, row_total, dotted)


def slot_backward(query_block, grad_block, log_block, delta_block, key_heads, value_heads):
    query_heads = split_heads(query_block)
    grad_heads = split_heads(grad_block)
    scores = jnp.einsum(
        "nqhd,nkhd->nqhk", query_heads, key_heads, preferred_element_type=jnp.float32
    ) * HEAD ** (-0.5)
    probabilities = jnp.exp(scores - log_block[..., None])
    grad_probs = jnp.einsum(
        "nqhd,nkhd->nqhk", grad_heads, value_heads, preferred_element_type=jnp.float32
    )
    grad_scores = (probabilities * (grad_probs - delta_block[..., None])).astype(jnp.bfloat16)
    grad_query = (
        jnp.einsum("nqhk,nkhd->nqhd", grad_scores, key_heads, preferred_element_type=jnp.float32)
        * HEAD ** (-0.5)
    ).astype(jnp.bfloat16)
    value_term = jnp.einsum(
        "nqhk,nqhd->nkhd",
        probabilities.astype(jnp.bfloat16),
        grad_heads,
        preferred_element_type=jnp.float32,
    )
    key_term = jnp.einsum(
        "nqhk,nqhd->nkhd", grad_scores, query_heads, preferred_element_type=jnp.float32
    )
    return (grad_query.reshape(query_block.shape), key_term, value_term)


def shards(queries, grad_out, neighbour_keys, neighbour_values, neighbours):
    groups = lax.axis_size("grp")
    span_len = SPAN
    tok_rows = queries.shape[1]
    row_width = queries.shape[2]
    neighbour_len = neighbour_keys.shape[2]
    span_count = tok_rows // span_len
    pair_count = span_count * NBRS
    capacity = (pair_count + groups - 1) // groups
    slot_count = groups * capacity
    score_scale = HEAD ** (-0.5)
    width = row_width // CHUNKS
    head_width = width // HEAD
    next_query, next_grad = from_behind(
        (queries[0, : span_len - 1], grad_out[0, : span_len - 1]), "seq", -1
    )
    window_query = jnp.concatenate([queries[0, span_len - 1 :], next_query], axis=0).reshape(
        span_count, span_len, row_width
    )
    window_grad = jnp.concatenate([grad_out[0, span_len - 1 :], next_grad], axis=0).reshape(
        span_count, span_len, row_width
    )
    owner_ids = neighbours[0].reshape(pair_count)
    group_ids = jnp.arange(groups, dtype=jnp.int32)
    owner_hits = (owner_ids[:, None] == group_ids[None, :]).astype(jnp.int32)
    earlier = jnp.cumsum(owner_hits, axis=0) - owner_hits
    slot_rank = jnp.sum(earlier * owner_hits, axis=1)
    slot_of = owner_ids * capacity + slot_rank
    slot_ids = jnp.arange(slot_count, dtype=jnp.int32)
    placement = (slot_of[None, :] == slot_ids[:, None]).astype(jnp.int32)
    slot_live = jnp.sum(placement, axis=1)
    slot_span = (
        jnp.sum(placement * jnp.arange(pair_count, dtype=jnp.int32)[None, :], axis=1) // NBRS
    )
    live_rows = slot_live[:, None, None] > 0
    slot_query = jnp.where(live_rows, window_query[slot_span], jnp.zeros((), queries.dtype))
    slot_grad = jnp.where(live_rows, window_grad[slot_span], jnp.zeros((), grad_out.dtype))
    key_block = neighbour_keys[0, 0]
    value_block = neighbour_values[0, 0]
    pair_shape = (span_count, NBRS, span_len, head_width)
    window_parts, key_parts, value_parts = [], [], []
    for chunk in range(CHUNKS):
        cols = slice(chunk * width, (chunk + 1) * width)
        key_all = lax.all_gather(key_block[:, cols], "grp", axis=0)
        value_all = lax.all_gather(value_block[:, cols], "grp", axis=0)
        key_heads = split_heads(jnp.repeat(key_all, capacity, axis=0))
        value_heads = split_heads(jnp.repeat(value_all, capacity, axis=0))
        query_part = slot_query[..., cols]
        grad_part = slot_grad[..., cols]
        stat_max, stat_total, stat_dot = slot_forward(query_part, grad_part, key_heads, value_heads)
        pair_max = stat_max[slot_of].reshape(pair_shape)
        pair_total = stat_total[slot_of].reshape(pair_shape)
        pair_dot = stat_dot[slot_of].reshape(pair_shape)
        top_max = jnp.max(pair_max, axis=1, keepdims=True)
        weights = pair_total * jnp.exp(pair_max - top_max)
        weight_sum = jnp.sum(weights, axis=1)
        log_total = top_max[:, 0] + jnp.log(weight_sum)
        delta_rows = jnp.sum(weights * pair_dot, axis=1) / weight_sum
        grad_query, key_term, value_term = slot_backward(
            query_part,
            grad_part,
            log_total[slot_span],
            delta_rows[slot_span],
            key_heads,
            value_heads,
        )
        pair_grad = grad_query[slot_of].reshape(span_count, NBRS, span_len, width)
        window_parts.append(jnp.sum(pair_grad.astype(jnp.float32), axis=1).astype(jnp.bfloat16))
        key_send = (
            jnp.sum(key_term.reshape(groups, capacity, neighbour_len, width), axis=1) * score_scale
        ).astype(jnp.bfloat16)
        value_send = jnp.sum(
            value_term.reshape(groups, capacity, neighbour_len, width), axis=1
        ).astype(jnp.bfloat16)
        key_parts.append(lax.psum_scatter(key_send, "grp", scatter_dimension=0, tiled=True))
        value_parts.append(lax.psum_scatter(value_send, "grp", scatter_dimension=0, tiled=True))
    grad_windows = jnp.concatenate(window_parts, axis=-1).reshape(
        1, span_count, span_len, row_width
    )
    grad_keys = jnp.concatenate(key_parts, axis=-1).reshape(1, 1, neighbour_len, row_width)
    grad_values = jnp.concatenate(value_parts, axis=-1).reshape(1, 1, neighbour_len, row_width)
    return (grad_windows, grad_keys, grad_values)


def solution(mesh):
    in_specs = (
        P("grp", "seq", None),
        P("grp", "seq", None),
        P("grp", "seq", None, None),
        P("grp", "seq", None, None),
        P("grp", "seq", None),
    )
    out_specs = (
        P("grp", "seq", None, None),
        P("grp", "seq", None, None),
        P("grp", "seq", None, None),
    )
    return jax.shard_map(shards, mesh=mesh, in_specs=in_specs, out_specs=out_specs, check_vma=False)
```

```python
import jax
import jax.numpy as jnp
from jax import lax
from jax.sharding import PartitionSpec as P

HEAD = 128
SPAN = 64
NBRS = 4
CHUNKS = 4


def from_behind(array, axis, by):
    length = lax.axis_size(axis)
    pairs = [(i, i + by) for i in range(length) if 0 <= i + by < length]
    return lax.ppermute(array, axis, pairs)


def split_heads(block_rows):
    return block_rows.reshape(block_rows.shape[:-1] + (block_rows.shape[-1] // HEAD, HEAD))


def slot_forward(query_block, grad_block, key_heads, value_heads):
    query_heads = split_heads(query_block)
    scores = jnp.einsum(
        "nqhd,nkhd->nqhk", query_heads, key_heads, preferred_element_type=jnp.float32
    ) * HEAD ** (-0.5)
    row_max = jnp.max(scores, axis=-1)
    exp_scores = jnp.exp(scores - row_max[..., None])
    row_total = jnp.sum(exp_scores, axis=-1)
    partial_value = (
        jnp.einsum(
            "nqhk,nkhd->nqhd",
            exp_scores.astype(jnp.bfloat16),
            value_heads,
            preferred_element_type=jnp.float32,
        )
        / row_total[..., None]
    )
    dotted = jnp.sum(split_heads(grad_block).astype(jnp.float32) * partial_value, axis=-1)
    return (row_max, row_total, dotted)


def slot_backward(query_block, grad_block, log_block, delta_block, key_heads, value_heads):
    query_heads = split_heads(query_block)
    grad_heads = split_heads(grad_block)
    scores = jnp.einsum(
        "nqhd,nkhd->nqhk", query_heads, key_heads, preferred_element_type=jnp.float32
    ) * HEAD ** (-0.5)
    probabilities = jnp.exp(scores - log_block[..., None])
    grad_probs = jnp.einsum(
        "nqhd,nkhd->nqhk", grad_heads, value_heads, preferred_element_type=jnp.float32
    )
    grad_scores = (probabilities * (grad_probs - delta_block[..., None])).astype(jnp.bfloat16)
    grad_query = (
        jnp.einsum("nqhk,nkhd->nqhd", grad_scores, key_heads, preferred_element_type=jnp.float32)
        * HEAD ** (-0.5)
    ).astype(jnp.bfloat16)
    value_term = jnp.einsum(
        "nqhk,nqhd->nkhd",
        probabilities.astype(jnp.bfloat16),
        grad_heads,
        preferred_element_type=jnp.float32,
    )
    key_term = jnp.einsum(
        "nqhk,nqhd->nkhd", grad_scores, query_heads, preferred_element_type=jnp.float32
    )
    return (grad_query.reshape(query_block.shape), key_term, value_term)


def ring_step(array, axis, by):
    length = lax.axis_size(axis)
    pairs = [(i, (i + by) % length) for i in range(length)]
    return lax.ppermute(array, axis, pairs)


def shards(queries, grad_out, neighbour_keys, neighbour_values, neighbours):
    groups = lax.axis_size("grp")
    me = lax.axis_index("grp")
    span_len = SPAN
    tok_rows = queries.shape[1]
    row_width = queries.shape[2]
    head_count = row_width // HEAD
    neighbour_len = neighbour_keys.shape[2]
    span_count = tok_rows // span_len
    pair_count = span_count * NBRS
    assert pair_count == groups
    score_scale = HEAD ** (-0.5)
    ahead = groups // 2
    behind = groups - 1 - ahead
    next_query, next_grad = from_behind(
        (queries[0, : span_len - 1], grad_out[0, : span_len - 1]), "seq", -1
    )
    window_query = jnp.concatenate([queries[0, span_len - 1 :], next_query], axis=0).reshape(
        span_count, span_len, row_width
    )
    window_grad = jnp.concatenate([grad_out[0, span_len - 1 :], next_grad], axis=0).reshape(
        span_count, span_len, row_width
    )
    owner_ids = neighbours[0].reshape(pair_count)
    group_ids = jnp.arange(groups, dtype=jnp.int32)
    placement = (owner_ids[None, :] == group_ids[:, None]).astype(jnp.int32)
    owner_span = jnp.sum(placement * jnp.arange(pair_count, dtype=jnp.int32)[None, :], axis=1) // NBRS
    rel_groups = (me + group_ids) % groups
    slot_span = owner_span[rel_groups]
    pair_slot = (owner_ids - me) % groups
    slot_query = window_query[slot_span]
    slot_grad = window_grad[slot_span]
    held = jnp.stack([neighbour_keys[0, 0], neighbour_values[0, 0]])
    ahead_blocks, behind_blocks = [], []
    going_up, going_down = held, held
    for step in range(1, ahead + 1):
        going_up = ring_step(going_up, "grp", 1)
        ahead_blocks.append(going_up)
        if step <= behind:
            going_down = ring_step(going_down, "grp", -1)
            behind_blocks.append(going_down)
    all_blocks = jnp.stack([held] + behind_blocks + ahead_blocks[::-1], axis=0)
    key_heads = split_heads(all_blocks[:, 0])
    value_heads = split_heads(all_blocks[:, 1])
    stat_max, stat_total, stat_dot = slot_forward(slot_query, slot_grad, key_heads, value_heads)
    pair_shape = (span_count, NBRS, span_len, head_count)
    pair_max = stat_max[pair_slot].reshape(pair_shape)
    pair_total = stat_total[pair_slot].reshape(pair_shape)
    pair_dot = stat_dot[pair_slot].reshape(pair_shape)
    top_max = jnp.max(pair_max, axis=1, keepdims=True)
    weights = pair_total * jnp.exp(pair_max - top_max)
    weight_sum = jnp.sum(weights, axis=1)
    log_total = top_max[:, 0] + jnp.log(weight_sum)
    delta_rows = jnp.sum(weights * pair_dot, axis=1) / weight_sum
    grad_query, key_term, value_term = slot_backward(
        slot_query,
        slot_grad,
        log_total[slot_span],
        delta_rows[slot_span],
        key_heads,
        value_heads,
    )
    pair_grad = grad_query[pair_slot].reshape(span_count, NBRS, span_len, row_width)
    grad_windows = (
        jnp.sum(pair_grad.astype(jnp.float32), axis=1)
        .astype(jnp.bfloat16)
        .reshape(1, span_count, span_len, row_width)
    )
    terms = jnp.stack(
        [key_term.reshape(groups, neighbour_len, row_width) * score_scale,
         value_term.reshape(groups, neighbour_len, row_width)],
        axis=1,
    ).astype(jnp.bfloat16)
    up_sum = terms[ahead]
    for step in range(1, ahead + 1):
        up_arrived = ring_step(up_sum, "grp", 1).astype(jnp.float32)
        if step < ahead:
            up_sum = (up_arrived + terms[ahead - step]).astype(jnp.bfloat16)
    down_sum = terms[groups - behind]
    for step in range(1, behind + 1):
        down_arrived = ring_step(down_sum, "grp", -1).astype(jnp.float32)
        if step < behind:
            down_sum = (down_arrived + terms[groups - behind + step]).astype(jnp.bfloat16)
    total = up_arrived + down_arrived + terms[0].astype(jnp.float32)
    grad_keys = total[0].astype(jnp.bfloat16).reshape(1, 1, neighbour_len, row_width)
    grad_values = total[1].astype(jnp.bfloat16).reshape(1, 1, neighbour_len, row_width)
    return (grad_windows, grad_keys, grad_values)


def solution(mesh):
    in_specs = (
        P("grp", "seq", None),
        P("grp", "seq", None),
        P("grp", "seq", None, None),
        P("grp", "seq", None, None),
        P("grp", "seq", None),
    )
    out_specs = (
        P("grp", "seq", None, None),
        P("grp", "seq", None, None),
        P("grp", "seq", None, None),
    )
    return jax.shard_map(shards, mesh=mesh, in_specs=in_specs, out_specs=out_specs, check_vma=False)
```

```python
import jax
import jax.numpy as jnp
from jax import lax
from jax.sharding import PartitionSpec as P

HEAD = 128
SPAN = 64
NBRS = 4
CHUNKS = 4


def from_behind(array, axis, by):
    length = lax.axis_size(axis)
    pairs = [(i, i + by) for i in range(length) if 0 <= i + by < length]
    return lax.ppermute(array, axis, pairs)


def split_heads(block_rows):
    return block_rows.reshape(block_rows.shape[:-1] + (block_rows.shape[-1] // HEAD, HEAD))


def slot_forward(query_block, grad_block, key_heads, value_heads):
    query_heads = split_heads(query_block)
    scores = jnp.einsum(
        "nqhd,nkhd->nqhk", query_heads, key_heads, preferred_element_type=jnp.float32
    ) * HEAD ** (-0.5)
    row_max = jnp.max(scores, axis=-1)
    exp_scores = jnp.exp(scores - row_max[..., None])
    row_total = jnp.sum(exp_scores, axis=-1)
    partial_value = (
        jnp.einsum(
            "nqhk,nkhd->nqhd",
            exp_scores.astype(jnp.bfloat16),
            value_heads,
            preferred_element_type=jnp.float32,
        )
        / row_total[..., None]
    )
    dotted = jnp.sum(split_heads(grad_block).astype(jnp.float32) * partial_value, axis=-1)
    return (row_max, row_total, dotted)


def slot_backward(query_block, grad_block, log_block, delta_block, key_heads, value_heads):
    query_heads = split_heads(query_block)
    grad_heads = split_heads(grad_block)
    scores = jnp.einsum(
        "nqhd,nkhd->nqhk", query_heads, key_heads, preferred_element_type=jnp.float32
    ) * HEAD ** (-0.5)
    probabilities = jnp.exp(scores - log_block[..., None])
    grad_probs = jnp.einsum(
        "nqhd,nkhd->nqhk", grad_heads, value_heads, preferred_element_type=jnp.float32
    )
    grad_scores = (probabilities * (grad_probs - delta_block[..., None])).astype(jnp.bfloat16)
    grad_query = (
        jnp.einsum("nqhk,nkhd->nqhd", grad_scores, key_heads, preferred_element_type=jnp.float32)
        * HEAD ** (-0.5)
    ).astype(jnp.bfloat16)
    value_term = jnp.einsum(
        "nqhk,nqhd->nkhd",
        probabilities.astype(jnp.bfloat16),
        grad_heads,
        preferred_element_type=jnp.float32,
    )
    key_term = jnp.einsum(
        "nqhk,nqhd->nkhd", grad_scores, query_heads, preferred_element_type=jnp.float32
    )
    return (grad_query.reshape(query_block.shape), key_term, value_term)


def ring_step(array, axis, by):
    length = lax.axis_size(axis)
    pairs = [(i, (i + by) % length) for i in range(length)]
    return lax.ppermute(array, axis, pairs)


def shards(queries, grad_out, neighbour_keys, neighbour_values, neighbours):
    groups = lax.axis_size("grp")
    me = lax.axis_index("grp")
    span_len = SPAN
    tok_rows = queries.shape[1]
    row_width = queries.shape[2]
    head_count = row_width // HEAD
    neighbour_len = neighbour_keys.shape[2]
    span_count = tok_rows // span_len
    pair_count = span_count * NBRS
    assert pair_count == groups
    score_scale = HEAD ** (-0.5)
    ahead = groups // 2
    behind = groups - 1 - ahead
    next_query, next_grad = from_behind(
        (queries[0, : span_len - 1], grad_out[0, : span_len - 1]), "seq", -1
    )
    window_query = jnp.concatenate([queries[0, span_len - 1 :], next_query], axis=0).reshape(
        span_count, span_len, row_width
    )
    window_grad = jnp.concatenate([grad_out[0, span_len - 1 :], next_grad], axis=0).reshape(
        span_count, span_len, row_width
    )
    owner_ids = neighbours[0].reshape(pair_count)
    group_ids = jnp.arange(groups, dtype=jnp.int32)
    placement = (owner_ids[None, :] == group_ids[:, None]).astype(jnp.int32)
    owner_span = jnp.sum(placement * jnp.arange(pair_count, dtype=jnp.int32)[None, :], axis=1) // NBRS
    rel_groups = (me + group_ids) % groups
    slot_span = owner_span[rel_groups]
    pair_slot = (owner_ids - me) % groups
    slot_query = window_query[slot_span]
    slot_grad = window_grad[slot_span]
    held = jnp.stack([neighbour_keys[0, 0], neighbour_values[0, 0]])
    ahead_blocks, behind_blocks = [], []
    going_up, going_down = held, held
    for step in range(1, ahead + 1):
        going_up = ring_step(going_up, "grp", 1)
        if step <= behind:
            going_down = ring_step(going_down, "grp", -1)
            going_up, going_down = lax.optimization_barrier((going_up, going_down))
            behind_blocks.append(going_down)
        ahead_blocks.append(going_up)
    all_blocks = jnp.stack([held] + behind_blocks + ahead_blocks[::-1], axis=0)
    key_heads = split_heads(all_blocks[:, 0])
    value_heads = split_heads(all_blocks[:, 1])
    stat_max, stat_total, stat_dot = slot_forward(slot_query, slot_grad, key_heads, value_heads)
    pair_shape = (span_count, NBRS, span_len, head_count)
    pair_max = stat_max[pair_slot].reshape(pair_shape)
    pair_total = stat_total[pair_slot].reshape(pair_shape)
    pair_dot = stat_dot[pair_slot].reshape(pair_shape)
    top_max = jnp.max(pair_max, axis=1, keepdims=True)
    weights = pair_total * jnp.exp(pair_max - top_max)
    weight_sum = jnp.sum(weights, axis=1)
    log_total = top_max[:, 0] + jnp.log(weight_sum)
    delta_rows = jnp.sum(weights * pair_dot, axis=1) / weight_sum
    grad_query, key_term, value_term = slot_backward(
        slot_query,
        slot_grad,
        log_total[slot_span],
        delta_rows[slot_span],
        key_heads,
        value_heads,
    )
    pair_grad = grad_query[pair_slot].reshape(span_count, NBRS, span_len, row_width)
    grad_windows = (
        jnp.sum(pair_grad.astype(jnp.float32), axis=1)
        .astype(jnp.bfloat16)
        .reshape(1, span_count, span_len, row_width)
    )
    terms = jnp.stack(
        [key_term.reshape(groups, neighbour_len, row_width) * score_scale,
         value_term.reshape(groups, neighbour_len, row_width)],
        axis=1,
    ).astype(jnp.bfloat16)
    up_sum = terms[ahead]
    down_sum = terms[groups - behind]
    for step in range(1, ahead + 1):
        up_arrived = ring_step(up_sum, "grp", 1).astype(jnp.float32)
        if step <= behind:
            down_arrived = ring_step(down_sum, "grp", -1).astype(jnp.float32)
            up_arrived, down_arrived = lax.optimization_barrier((up_arrived, down_arrived))
        if step < ahead:
            up_sum = (up_arrived + terms[ahead - step]).astype(jnp.bfloat16)
        if step < behind:
            down_sum = (down_arrived + terms[groups - behind + step]).astype(jnp.bfloat16)
    total = up_arrived + down_arrived + terms[0].astype(jnp.float32)
    grad_keys = total[0].astype(jnp.bfloat16).reshape(1, 1, neighbour_len, row_width)
    grad_values = total[1].astype(jnp.bfloat16).reshape(1, 1, neighbour_len, row_width)
    return (grad_windows, grad_keys, grad_values)


def solution(mesh):
    in_specs = (
        P("grp", "seq", None),
        P("grp", "seq", None),
        P("grp", "seq", None, None),
        P("grp", "seq", None, None),
        P("grp", "seq", None),
    )
    out_specs = (
        P("grp", "seq", None, None),
        P("grp", "seq", None, None),
        P("grp", "seq", None, None),
    )
    return jax.shard_map(shards, mesh=mesh, in_specs=in_specs, out_specs=out_specs, check_vma=False)
```

```python
import jax
import jax.numpy as jnp
from jax import lax
from jax.experimental import pallas as pl
from jax.experimental.pallas import tpu as pltpu
from jax.sharding import PartitionSpec as P

HEAD = 128
SPAN = 64
NBRS = 4


def from_behind(array, axis, by):
    length = lax.axis_size(axis)
    pairs = [(i, i + by) for i in range(length) if 0 <= i + by < length]
    return lax.ppermute(array, axis, pairs)


def span_kernel(slot_ref, query_ref, grad_ref, *refs):
    key_refs = refs[:NBRS]
    value_refs = refs[NBRS : 2 * NBRS]
    window_ref, term_ref = refs[2 * NBRS :]
    scale = HEAD ** (-0.5)
    query = query_ref[0]
    grad = grad_ref[0]
    keys = jnp.concatenate([ref[0, 0] for ref in key_refs], axis=0)
    values = jnp.concatenate([ref[0, 0] for ref in value_refs], axis=0)
    contract_last = (((1,), (1,)), ((), ()))
    scores = lax.dot_general(query, keys, contract_last, preferred_element_type=jnp.float32) * scale
    grad_probs = lax.dot_general(grad, values, contract_last, preferred_element_type=jnp.float32)
    maxes, totals, dots = [], [], []
    for j in range(NBRS):
        part = scores[:, j * HEAD : (j + 1) * HEAD]
        row_max = jnp.max(part, axis=-1, keepdims=True)
        exp_part = jnp.exp(part - row_max)
        row_total = jnp.sum(exp_part, axis=-1, keepdims=True)
        rounded = exp_part.astype(jnp.bfloat16).astype(jnp.float32)
        dotted = jnp.sum(rounded * grad_probs[:, j * HEAD : (j + 1) * HEAD], axis=-1, keepdims=True)
        maxes.append(row_max)
        totals.append(row_total)
        dots.append(dotted / row_total)
    top = maxes[0]
    for j in range(1, NBRS):
        top = jnp.maximum(top, maxes[j])
    weights = [totals[j] * jnp.exp(maxes[j] - top) for j in range(NBRS)]
    weight_sum = weights[0] + weights[1] + weights[2] + weights[3]
    weighted = weights[0] * dots[0] + weights[1] * dots[1] + weights[2] * dots[2] + weights[3] * dots[3]
    log_total = top + jnp.log(weight_sum)
    delta = weighted / weight_sum
    probs = jnp.exp(scores - log_total)
    grad_scores = (probs * (grad_probs - delta)).astype(jnp.bfloat16)
    window = jnp.zeros(query.shape, jnp.float32)
    for j in range(NBRS):
        part = lax.dot_general(
            grad_scores[:, j * HEAD : (j + 1) * HEAD],
            keys[j * HEAD : (j + 1) * HEAD],
            (((1,), (0,)), ((), ())),
            preferred_element_type=jnp.float32,
        )
        window = window + (part * scale).astype(jnp.bfloat16).astype(jnp.float32)
    window_ref[0] = window.astype(window_ref.dtype)
    probs_t = probs.astype(jnp.bfloat16).astype(jnp.float32).T.astype(jnp.bfloat16)
    scores_t = grad_scores.astype(jnp.float32).T.astype(jnp.bfloat16)
    plain = (((1,), (0,)), ((), ()))
    value_term = lax.dot_general(probs_t, grad, plain, preferred_element_type=jnp.float32)
    key_term = lax.dot_general(scores_t, query, plain, preferred_element_type=jnp.float32) * scale
    for j in range(NBRS):
        term_ref[j, 0] = key_term[j * HEAD : (j + 1) * HEAD].astype(term_ref.dtype)
        term_ref[j, 1] = value_term[j * HEAD : (j + 1) * HEAD].astype(term_ref.dtype)


def span_attention(pair_slot, window_query, window_grad, blocks):
    span_count, span_len, row_width = window_query.shape
    slot_count, _, block_len, _ = blocks.shape
    head_count = row_width // HEAD
    pair_count = span_count * NBRS

    def window_map(h, i, slots):
        return (i, 0, h)

    def block_map(j, kind):
        return lambda h, i, slots: (slots[i * NBRS + j], kind, 0, h)

    in_specs = [
        pl.BlockSpec((1, span_len, HEAD), window_map),
        pl.BlockSpec((1, span_len, HEAD), window_map),
    ]
    in_specs += [pl.BlockSpec((1, 1, block_len, HEAD), block_map(j, 0)) for j in range(NBRS)]
    in_specs += [pl.BlockSpec((1, 1, block_len, HEAD), block_map(j, 1)) for j in range(NBRS)]
    out_specs = [
        pl.BlockSpec((1, span_len, HEAD), window_map),
        pl.BlockSpec((NBRS, 2, block_len, HEAD), lambda h, i, slots: (i, 0, 0, h)),
    ]
    flops = 2 * span_len * block_len * HEAD * 9 * pair_count * head_count
    return pl.pallas_call(
        span_kernel,
        grid_spec=pltpu.PrefetchScalarGridSpec(
            num_scalar_prefetch=1,
            grid=(head_count, span_count),
            in_specs=in_specs,
            out_specs=out_specs,
        ),
        out_shape=[
            jax.ShapeDtypeStruct((span_count, span_len, row_width), jnp.bfloat16),
            jax.ShapeDtypeStruct((pair_count, 2, block_len, row_width), jnp.bfloat16),
        ],
        cost_estimate=pl.CostEstimate(
            flops=flops,
            transcendentals=2 * pair_count * span_len * block_len * head_count,
            bytes_accessed=2 * (3 * blocks.size + 4 * window_query.size),
        ),
    )(pair_slot, window_query, window_grad, *([blocks] * (2 * NBRS)))


def ring_step(array, axis, by):
    length = lax.axis_size(axis)
    pairs = [(i, (i + by) % length) for i in range(length)]
    return lax.ppermute(array, axis, pairs)


def shards(queries, grad_out, neighbour_keys, neighbour_values, neighbours):
    groups = lax.axis_size("grp")
    me = lax.axis_index("grp")
    span_len = SPAN
    tok_rows = queries.shape[1]
    row_width = queries.shape[2]
    head_count = row_width // HEAD
    neighbour_len = neighbour_keys.shape[2]
    span_count = tok_rows // span_len
    pair_count = span_count * NBRS
    assert pair_count == groups
    score_scale = HEAD ** (-0.5)
    ahead = groups // 2
    behind = groups - 1 - ahead
    next_query, next_grad = from_behind(
        (queries[0, : span_len - 1], grad_out[0, : span_len - 1]), "seq", -1
    )
    window_query = jnp.concatenate([queries[0, span_len - 1 :], next_query], axis=0).reshape(
        span_count, span_len, row_width
    )
    window_grad = jnp.concatenate([grad_out[0, span_len - 1 :], next_grad], axis=0).reshape(
        span_count, span_len, row_width
    )
    owner_ids = neighbours[0].reshape(pair_count)
    group_ids = jnp.arange(groups, dtype=jnp.int32)
    placement = (owner_ids[None, :] == group_ids[:, None]).astype(jnp.int32)
    rel_groups = (me + group_ids) % groups
    pair_slot = (owner_ids - me) % groups
    held = jnp.stack([neighbour_keys[0, 0], neighbour_values[0, 0]])
    ahead_blocks, behind_blocks = [], []
    going_up, going_down = held, held
    for step in range(1, ahead + 1):
        going_up = ring_step(going_up, "grp", 1)
        if step <= behind:
            going_down = ring_step(going_down, "grp", -1)
            going_up, going_down = lax.optimization_barrier((going_up, going_down))
            behind_blocks.append(going_down)
        ahead_blocks.append(going_up)
    all_blocks = jnp.stack([held] + behind_blocks + ahead_blocks[::-1], axis=0)
    grad_windows, pair_terms = span_attention(pair_slot, window_query, window_grad, all_blocks)
    grad_windows = grad_windows.reshape(1, span_count, span_len, row_width)
    slot_pair = jnp.sum(placement * jnp.arange(pair_count, dtype=jnp.int32)[None, :], axis=1)
    slot_pair = slot_pair[rel_groups]

    def terms(slot):
        return lax.dynamic_index_in_dim(pair_terms, slot_pair[slot], axis=0, keepdims=False)

    up_sum = terms(ahead)
    down_sum = terms(groups - behind)
    for step in range(1, ahead + 1):
        up_arrived = ring_step(up_sum, "grp", 1).astype(jnp.float32)
        if step <= behind:
            down_arrived = ring_step(down_sum, "grp", -1).astype(jnp.float32)
            up_arrived, down_arrived = lax.optimization_barrier((up_arrived, down_arrived))
        if step < ahead:
            up_sum = (up_arrived + terms(ahead - step)).astype(jnp.bfloat16)
        if step < behind:
            down_sum = (down_arrived + terms(groups - behind + step)).astype(jnp.bfloat16)
    total = up_arrived + down_arrived + terms(0).astype(jnp.float32)
    grad_keys = total[0].astype(jnp.bfloat16).reshape(1, 1, neighbour_len, row_width)
    grad_values = total[1].astype(jnp.bfloat16).reshape(1, 1, neighbour_len, row_width)
    return (grad_windows, grad_keys, grad_values)


def solution(mesh):
    in_specs = (
        P("grp", "seq", None),
        P("grp", "seq", None),
        P("grp", "seq", None, None),
        P("grp", "seq", None, None),
        P("grp", "seq", None),
    )
    out_specs = (
        P("grp", "seq", None, None),
        P("grp", "seq", None, None),
        P("grp", "seq", None, None),
    )
    return jax.shard_map(shards, mesh=mesh, in_specs=in_specs, out_specs=out_specs, check_vma=False)
```

```python
import jax
import jax.numpy as jnp
from jax import lax
from jax.experimental import pallas as pl
from jax.experimental.pallas import tpu as pltpu
from jax.sharding import PartitionSpec as P

HEAD = 128
SPAN = 64
NBRS = 4


def from_behind(array, axis, by):
    length = lax.axis_size(axis)
    pairs = [(i, i + by) for i in range(length) if 0 <= i + by < length]
    return lax.ppermute(array, axis, pairs)


def span_kernel(slot_ref, query_ref, grad_ref, *refs):
    key_refs = refs[:NBRS]
    value_refs = refs[NBRS : 2 * NBRS]
    window_ref, term_ref = refs[2 * NBRS :]
    scale = HEAD ** (-0.5)
    query = query_ref[0]
    grad = grad_ref[0]
    keys = jnp.concatenate([ref[0, 0] for ref in key_refs], axis=0)
    values = jnp.concatenate([ref[0, 0] for ref in value_refs], axis=0)
    contract_last = (((1,), (1,)), ((), ()))
    scores = lax.dot_general(query, keys, contract_last, preferred_element_type=jnp.float32) * scale
    grad_probs = lax.dot_general(grad, values, contract_last, preferred_element_type=jnp.float32)
    maxes, totals, dots = [], [], []
    for j in range(NBRS):
        part = scores[:, j * HEAD : (j + 1) * HEAD]
        row_max = jnp.max(part, axis=-1, keepdims=True)
        exp_part = jnp.exp(part - row_max)
        row_total = jnp.sum(exp_part, axis=-1, keepdims=True)
        rounded = exp_part.astype(jnp.bfloat16).astype(jnp.float32)
        dotted = jnp.sum(rounded * grad_probs[:, j * HEAD : (j + 1) * HEAD], axis=-1, keepdims=True)
        maxes.append(row_max)
        totals.append(row_total)
        dots.append(dotted / row_total)
    top = maxes[0]
    for j in range(1, NBRS):
        top = jnp.maximum(top, maxes[j])
    weights = [totals[j] * jnp.exp(maxes[j] - top) for j in range(NBRS)]
    weight_sum = weights[0] + weights[1] + weights[2] + weights[3]
    weighted = weights[0] * dots[0] + weights[1] * dots[1] + weights[2] * dots[2] + weights[3] * dots[3]
    log_total = top + jnp.log(weight_sum)
    delta = weighted / weight_sum
    probs = jnp.exp(scores - log_total)
    grad_scores = (probs * (grad_probs - delta)).astype(jnp.bfloat16)
    window = jnp.zeros(query.shape, jnp.float32)
    for j in range(NBRS):
        part = lax.dot_general(
            grad_scores[:, j * HEAD : (j + 1) * HEAD],
            keys[j * HEAD : (j + 1) * HEAD],
            (((1,), (0,)), ((), ())),
            preferred_element_type=jnp.float32,
        )
        window = window + (part * scale).astype(jnp.bfloat16).astype(jnp.float32)
    window_ref[0] = window.astype(window_ref.dtype)
    probs_t = probs.astype(jnp.bfloat16).astype(jnp.float32).T.astype(jnp.bfloat16)
    scores_t = grad_scores.astype(jnp.float32).T.astype(jnp.bfloat16)
    plain = (((1,), (0,)), ((), ()))
    value_term = lax.dot_general(probs_t, grad, plain, preferred_element_type=jnp.float32)
    key_term = lax.dot_general(scores_t, query, plain, preferred_element_type=jnp.float32) * scale
    for j in range(NBRS):
        term_ref[j, 0] = key_term[j * HEAD : (j + 1) * HEAD].astype(term_ref.dtype)
        term_ref[j, 1] = value_term[j * HEAD : (j + 1) * HEAD].astype(term_ref.dtype)


def span_attention(pair_slot, window_query, window_grad, blocks):
    span_count, span_len, row_width = window_query.shape
    slot_count, _, block_len, _ = blocks.shape
    head_count = row_width // HEAD
    pair_count = span_count * NBRS

    def window_map(h, i, slots):
        return (i, 0, h)

    def block_map(j, kind):
        return lambda h, i, slots: (slots[i * NBRS + j], kind, 0, h)

    in_specs = [
        pl.BlockSpec((1, span_len, HEAD), window_map),
        pl.BlockSpec((1, span_len, HEAD), window_map),
    ]
    in_specs += [pl.BlockSpec((1, 1, block_len, HEAD), block_map(j, 0)) for j in range(NBRS)]
    in_specs += [pl.BlockSpec((1, 1, block_len, HEAD), block_map(j, 1)) for j in range(NBRS)]
    out_specs = [
        pl.BlockSpec((1, span_len, HEAD), window_map),
        pl.BlockSpec((NBRS, 2, block_len, HEAD), lambda h, i, slots: (i, 0, 0, h)),
    ]
    flops = 2 * span_len * block_len * HEAD * 9 * pair_count * head_count
    return pl.pallas_call(
        span_kernel,
        grid_spec=pltpu.PrefetchScalarGridSpec(
            num_scalar_prefetch=1,
            grid=(head_count, span_count),
            in_specs=in_specs,
            out_specs=out_specs,
        ),
        out_shape=[
            jax.ShapeDtypeStruct((span_count, span_len, row_width), jnp.bfloat16),
            jax.ShapeDtypeStruct((pair_count, 2, block_len, row_width), jnp.bfloat16),
        ],
        cost_estimate=pl.CostEstimate(
            flops=flops,
            transcendentals=2 * pair_count * span_len * block_len * head_count,
            bytes_accessed=2 * (3 * blocks.size + 4 * window_query.size),
        ),
    )(pair_slot, window_query, window_grad, *([blocks] * (2 * NBRS)))


def gather_kernel(held_ref, out_ref, send_sem, recv_sem, local_sem):
    groups = lax.axis_size("grp")
    me = lax.axis_index("grp")
    column = lax.axis_index("seq")
    ahead = groups // 2
    behind = groups - 1 - ahead
    up = lax.rem(me + 1, groups)
    down = lax.rem(me + groups - 1, groups)
    barrier = pltpu.get_barrier_semaphore()
    for neighbour in (up, down):
        pl.semaphore_signal(
            barrier, 1, device_id=(neighbour, column), device_id_type=pl.DeviceIdType.MESH
        )
    pl.semaphore_wait(barrier, 2)
    local = pltpu.make_async_copy(held_ref, out_ref.at[0], local_sem)
    local.start()
    for step in range(1, ahead + 1):
        copies = [
            pltpu.make_async_remote_copy(
                src_ref=held_ref if step == 1 else out_ref.at[groups + 1 - step],
                dst_ref=out_ref.at[groups - step],
                send_sem=send_sem.at[0, step - 1],
                recv_sem=recv_sem.at[0, step - 1],
                device_id=(up, column),
                device_id_type=pl.DeviceIdType.MESH,
            )
        ]
        if step <= behind:
            copies.append(
                pltpu.make_async_remote_copy(
                    src_ref=held_ref if step == 1 else out_ref.at[step - 1],
                    dst_ref=out_ref.at[step],
                    send_sem=send_sem.at[1, step - 1],
                    recv_sem=recv_sem.at[1, step - 1],
                    device_id=(down, column),
                    device_id_type=pl.DeviceIdType.MESH,
                )
            )
        for copy in copies:
            copy.start()
        for copy in copies:
            copy.wait()
    local.wait()


def ring_gather(held, groups):
    ahead = groups // 2
    return pl.pallas_call(
        gather_kernel,
        out_shape=jax.ShapeDtypeStruct((groups,) + held.shape, held.dtype),
        in_specs=[pl.BlockSpec(memory_space=pl.ANY)],
        out_specs=pl.BlockSpec(memory_space=pl.ANY),
        scratch_shapes=[
            pltpu.SemaphoreType.DMA((2, ahead)),
            pltpu.SemaphoreType.DMA((2, ahead)),
            pltpu.SemaphoreType.DMA(()),
        ],
        compiler_params=pltpu.CompilerParams(collective_id=0, has_side_effects=True),
    )(held)


def ring_step(array, axis, by):
    length = lax.axis_size(axis)
    pairs = [(i, (i + by) % length) for i in range(length)]
    return lax.ppermute(array, axis, pairs)


def shards(queries, grad_out, neighbour_keys, neighbour_values, neighbours):
    groups = lax.axis_size("grp")
    me = lax.axis_index("grp")
    span_len = SPAN
    tok_rows = queries.shape[1]
    row_width = queries.shape[2]
    head_count = row_width // HEAD
    neighbour_len = neighbour_keys.shape[2]
    span_count = tok_rows // span_len
    pair_count = span_count * NBRS
    assert pair_count == groups
    score_scale = HEAD ** (-0.5)
    ahead = groups // 2
    behind = groups - 1 - ahead
    next_query, next_grad = from_behind(
        (queries[0, : span_len - 1], grad_out[0, : span_len - 1]), "seq", -1
    )
    window_query = jnp.concatenate([queries[0, span_len - 1 :], next_query], axis=0).reshape(
        span_count, span_len, row_width
    )
    window_grad = jnp.concatenate([grad_out[0, span_len - 1 :], next_grad], axis=0).reshape(
        span_count, span_len, row_width
    )
    owner_ids = neighbours[0].reshape(pair_count)
    group_ids = jnp.arange(groups, dtype=jnp.int32)
    placement = (owner_ids[None, :] == group_ids[:, None]).astype(jnp.int32)
    rel_groups = (me + group_ids) % groups
    pair_slot = (owner_ids - me) % groups
    held = jnp.stack([neighbour_keys[0, 0], neighbour_values[0, 0]])
    all_blocks = ring_gather(held, groups)
    grad_windows, pair_terms = span_attention(pair_slot, window_query, window_grad, all_blocks)
    grad_windows = grad_windows.reshape(1, span_count, span_len, row_width)
    slot_pair = jnp.sum(placement * jnp.arange(pair_count, dtype=jnp.int32)[None, :], axis=1)
    slot_pair = slot_pair[rel_groups]

    def terms(slot):
        return lax.dynamic_index_in_dim(pair_terms, slot_pair[slot], axis=0, keepdims=False)

    up_sum = terms(ahead)
    down_sum = terms(groups - behind)
    for step in range(1, ahead + 1):
        up_arrived = ring_step(up_sum, "grp", 1).astype(jnp.float32)
        if step <= behind:
            down_arrived = ring_step(down_sum, "grp", -1).astype(jnp.float32)
            up_arrived, down_arrived = lax.optimization_barrier((up_arrived, down_arrived))
        if step < ahead:
            up_sum = (up_arrived + terms(ahead - step)).astype(jnp.bfloat16)
        if step < behind:
            down_sum = (down_arrived + terms(groups - behind + step)).astype(jnp.bfloat16)
    total = up_arrived + down_arrived + terms(0).astype(jnp.float32)
    grad_keys = total[0].astype(jnp.bfloat16).reshape(1, 1, neighbour_len, row_width)
    grad_values = total[1].astype(jnp.bfloat16).reshape(1, 1, neighbour_len, row_width)
    return (grad_windows, grad_keys, grad_values)


def solution(mesh):
    in_specs = (
        P("grp", "seq", None),
        P("grp", "seq", None),
        P("grp", "seq", None, None),
        P("grp", "seq", None, None),
        P("grp", "seq", None),
    )
    out_specs = (
        P("grp", "seq", None, None),
        P("grp", "seq", None, None),
        P("grp", "seq", None, None),
    )
    return jax.shard_map(shards, mesh=mesh, in_specs=in_specs, out_specs=out_specs, check_vma=False)
```

```python
import jax
import jax.numpy as jnp
from jax import lax
from jax.experimental import pallas as pl
from jax.experimental.pallas import tpu as pltpu
from jax.sharding import PartitionSpec as P

HEAD = 128
SPAN = 64
NBRS = 4


def from_behind(array, axis, by):
    length = lax.axis_size(axis)
    pairs = [(i, i + by) for i in range(length) if 0 <= i + by < length]
    return lax.ppermute(array, axis, pairs)


def span_kernel(slot_ref, query_ref, grad_ref, block_ref, window_ref, term_ref):
    scale = HEAD ** (-0.5)
    contract_last = (((1,), (1,)), ((), ()))
    plain = (((1,), (0,)), ((), ()))
    for span in range(query_ref.shape[0]):
        query = query_ref[span]
        grad = grad_ref[span]
        slots = [slot_ref[span * NBRS + j] for j in range(NBRS)]
        keys = jnp.concatenate([block_ref[slot, 0] for slot in slots], axis=0)
        values = jnp.concatenate([block_ref[slot, 1] for slot in slots], axis=0)
        scores = lax.dot_general(query, keys, contract_last, preferred_element_type=jnp.float32) * scale
        grad_probs = lax.dot_general(grad, values, contract_last, preferred_element_type=jnp.float32)
        maxes, totals, dots = [], [], []
        for j in range(NBRS):
            part = scores[:, j * HEAD : (j + 1) * HEAD]
            row_max = jnp.max(part, axis=-1, keepdims=True)
            exp_part = jnp.exp(part - row_max)
            row_total = jnp.sum(exp_part, axis=-1, keepdims=True)
            rounded = exp_part.astype(jnp.bfloat16).astype(jnp.float32)
            dotted = jnp.sum(
                rounded * grad_probs[:, j * HEAD : (j + 1) * HEAD], axis=-1, keepdims=True
            )
            maxes.append(row_max)
            totals.append(row_total)
            dots.append(dotted / row_total)
        top = maxes[0]
        for j in range(1, NBRS):
            top = jnp.maximum(top, maxes[j])
        weights = [totals[j] * jnp.exp(maxes[j] - top) for j in range(NBRS)]
        weight_sum = weights[0]
        weighted = weights[0] * dots[0]
        for j in range(1, NBRS):
            weight_sum = weight_sum + weights[j]
            weighted = weighted + weights[j] * dots[j]
        log_total = top + jnp.log(weight_sum)
        delta = weighted / weight_sum
        probs = jnp.exp(scores - log_total)
        grad_scores = (probs * (grad_probs - delta)).astype(jnp.bfloat16)
        window = jnp.zeros(query.shape, jnp.float32)
        for j in range(NBRS):
            part = lax.dot_general(
                grad_scores[:, j * HEAD : (j + 1) * HEAD],
                keys[j * HEAD : (j + 1) * HEAD],
                plain,
                preferred_element_type=jnp.float32,
            )
            window = window + (part * scale).astype(jnp.bfloat16).astype(jnp.float32)
        window_ref[span] = window.astype(window_ref.dtype)
        probs_t = probs.astype(jnp.bfloat16).astype(jnp.float32).T.astype(jnp.bfloat16)
        scores_t = grad_scores.astype(jnp.float32).T.astype(jnp.bfloat16)
        value_term = lax.dot_general(probs_t, grad, plain, preferred_element_type=jnp.float32)
        key_term = lax.dot_general(scores_t, query, plain, preferred_element_type=jnp.float32) * scale
        for j in range(NBRS):
            term_ref[span * NBRS + j, 0] = key_term[j * HEAD : (j + 1) * HEAD].astype(term_ref.dtype)
            term_ref[span * NBRS + j, 1] = value_term[j * HEAD : (j + 1) * HEAD].astype(term_ref.dtype)


def span_attention(pair_slot, window_query, window_grad, blocks):
    span_count, span_len, row_width = window_query.shape
    slot_count, _, block_len, _ = blocks.shape
    head_count = row_width // HEAD
    pair_count = span_count * NBRS

    def window_map(h, slots):
        return (0, 0, h)

    def block_map(h, slots):
        return (0, 0, 0, h)

    flops = 2 * span_len * block_len * HEAD * 9 * pair_count * head_count
    return pl.pallas_call(
        span_kernel,
        grid_spec=pltpu.PrefetchScalarGridSpec(
            num_scalar_prefetch=1,
            grid=(head_count,),
            in_specs=[
                pl.BlockSpec((span_count, span_len, HEAD), window_map),
                pl.BlockSpec((span_count, span_len, HEAD), window_map),
                pl.BlockSpec((slot_count, 2, block_len, HEAD), block_map),
            ],
            out_specs=[
                pl.BlockSpec((span_count, span_len, HEAD), window_map),
                pl.BlockSpec((pair_count, 2, block_len, HEAD), block_map),
            ],
        ),
        out_shape=[
            jax.ShapeDtypeStruct((span_count, span_len, row_width), jnp.bfloat16),
            jax.ShapeDtypeStruct((pair_count, 2, block_len, row_width), jnp.bfloat16),
        ],
        cost_estimate=pl.CostEstimate(
            flops=flops,
            transcendentals=2 * pair_count * span_len * block_len * head_count,
            bytes_accessed=2 * (2 * blocks.size + 3 * window_query.size),
        ),
    )(pair_slot, window_query, window_grad, blocks)


def gather_kernel(held_ref, out_ref, send_sem, recv_sem, local_sem):
    groups = lax.axis_size("grp")
    me = lax.axis_index("grp")
    column = lax.axis_index("seq")
    ahead = groups // 2
    behind = groups - 1 - ahead
    up = lax.rem(me + 1, groups)
    down = lax.rem(me + groups - 1, groups)
    barrier = pltpu.get_barrier_semaphore()
    for neighbour in (up, down):
        pl.semaphore_signal(
            barrier, 1, device_id=(neighbour, column), device_id_type=pl.DeviceIdType.MESH
        )
    pl.semaphore_wait(barrier, 2)
    local = pltpu.make_async_copy(held_ref, out_ref.at[0], local_sem)
    local.start()
    for step in range(1, ahead + 1):
        copies = [
            pltpu.make_async_remote_copy(
                src_ref=held_ref if step == 1 else out_ref.at[groups + 1 - step],
                dst_ref=out_ref.at[groups - step],
                send_sem=send_sem.at[0, step - 1],
                recv_sem=recv_sem.at[0, step - 1],
                device_id=(up, column),
                device_id_type=pl.DeviceIdType.MESH,
            )
        ]
        if step <= behind:
            copies.append(
                pltpu.make_async_remote_copy(
                    src_ref=held_ref if step == 1 else out_ref.at[step - 1],
                    dst_ref=out_ref.at[step],
                    send_sem=send_sem.at[1, step - 1],
                    recv_sem=recv_sem.at[1, step - 1],
                    device_id=(down, column),
                    device_id_type=pl.DeviceIdType.MESH,
                )
            )
        for copy in copies:
            copy.start()
        for copy in copies:
            copy.wait()
    local.wait()


def ring_gather(held, groups):
    ahead = groups // 2
    return pl.pallas_call(
        gather_kernel,
        out_shape=jax.ShapeDtypeStruct((groups,) + held.shape, held.dtype),
        in_specs=[pl.BlockSpec(memory_space=pl.ANY)],
        out_specs=pl.BlockSpec(memory_space=pl.ANY),
        scratch_shapes=[
            pltpu.SemaphoreType.DMA((2, ahead)),
            pltpu.SemaphoreType.DMA((2, ahead)),
            pltpu.SemaphoreType.DMA(()),
        ],
        compiler_params=pltpu.CompilerParams(collective_id=0, has_side_effects=True),
    )(held)


def ring_step(array, axis, by):
    length = lax.axis_size(axis)
    pairs = [(i, (i + by) % length) for i in range(length)]
    return lax.ppermute(array, axis, pairs)


def shards(queries, grad_out, neighbour_keys, neighbour_values, neighbours):
    groups = lax.axis_size("grp")
    me = lax.axis_index("grp")
    span_len = SPAN
    tok_rows = queries.shape[1]
    row_width = queries.shape[2]
    head_count = row_width // HEAD
    neighbour_len = neighbour_keys.shape[2]
    span_count = tok_rows // span_len
    pair_count = span_count * NBRS
    assert pair_count == groups
    score_scale = HEAD ** (-0.5)
    ahead = groups // 2
    behind = groups - 1 - ahead
    next_query, next_grad = from_behind(
        (queries[0, : span_len - 1], grad_out[0, : span_len - 1]), "seq", -1
    )
    window_query = jnp.concatenate([queries[0, span_len - 1 :], next_query], axis=0).reshape(
        span_count, span_len, row_width
    )
    window_grad = jnp.concatenate([grad_out[0, span_len - 1 :], next_grad], axis=0).reshape(
        span_count, span_len, row_width
    )
    owner_ids = neighbours[0].reshape(pair_count)
    group_ids = jnp.arange(groups, dtype=jnp.int32)
    placement = (owner_ids[None, :] == group_ids[:, None]).astype(jnp.int32)
    rel_groups = (me + group_ids) % groups
    pair_slot = (owner_ids - me) % groups
    held = jnp.stack([neighbour_keys[0, 0], neighbour_values[0, 0]])
    all_blocks = ring_gather(held, groups)
    grad_windows, pair_terms = span_attention(pair_slot, window_query, window_grad, all_blocks)
    grad_windows = grad_windows.reshape(1, span_count, span_len, row_width)
    slot_pair = jnp.sum(placement * jnp.arange(pair_count, dtype=jnp.int32)[None, :], axis=1)
    slot_pair = slot_pair[rel_groups]

    def terms(slot):
        return lax.dynamic_index_in_dim(pair_terms, slot_pair[slot], axis=0, keepdims=False)

    up_sum = terms(ahead)
    down_sum = terms(groups - behind)
    for step in range(1, ahead + 1):
        up_arrived = ring_step(up_sum, "grp", 1).astype(jnp.float32)
        if step <= behind:
            down_arrived = ring_step(down_sum, "grp", -1).astype(jnp.float32)
            up_arrived, down_arrived = lax.optimization_barrier((up_arrived, down_arrived))
        if step < ahead:
            up_sum = (up_arrived + terms(ahead - step)).astype(jnp.bfloat16)
        if step < behind:
            down_sum = (down_arrived + terms(groups - behind + step)).astype(jnp.bfloat16)
    total = up_arrived + down_arrived + terms(0).astype(jnp.float32)
    grad_keys = total[0].astype(jnp.bfloat16).reshape(1, 1, neighbour_len, row_width)
    grad_values = total[1].astype(jnp.bfloat16).reshape(1, 1, neighbour_len, row_width)
    return (grad_windows, grad_keys, grad_values)


def solution(mesh):
    in_specs = (
        P("grp", "seq", None),
        P("grp", "seq", None),
        P("grp", "seq", None, None),
        P("grp", "seq", None, None),
        P("grp", "seq", None),
    )
    out_specs = (
        P("grp", "seq", None, None),
        P("grp", "seq", None, None),
        P("grp", "seq", None, None),
    )
    return jax.shard_map(shards, mesh=mesh, in_specs=in_specs, out_specs=out_specs, check_vma=False)
```

```python
import jax
import jax.numpy as jnp
from jax import lax
from jax.experimental import pallas as pl
from jax.experimental.pallas import tpu as pltpu
from jax.sharding import PartitionSpec as P

HEAD = 128
SPAN = 64
NBRS = 4


def from_behind(array, axis, by):
    length = lax.axis_size(axis)
    pairs = [(i, i + by) for i in range(length) if 0 <= i + by < length]
    return lax.ppermute(array, axis, pairs)


def span_kernel(slot_ref, query_ref, grad_ref, block_ref, window_ref, term_ref):
    scale = HEAD ** (-0.5)
    contract_last = (((1,), (1,)), ((), ()))
    plain = (((1,), (0,)), ((), ()))
    for span in range(query_ref.shape[0]):
        query = query_ref[span]
        grad = grad_ref[span]
        slots = [slot_ref[span * NBRS + j] for j in range(NBRS)]
        keys = jnp.concatenate([block_ref[slot, 0] for slot in slots], axis=0)
        values = jnp.concatenate([block_ref[slot, 1] for slot in slots], axis=0)
        scores = lax.dot_general(query, keys, contract_last, preferred_element_type=jnp.float32) * scale
        grad_probs = lax.dot_general(grad, values, contract_last, preferred_element_type=jnp.float32)
        maxes, totals, dots = [], [], []
        for j in range(NBRS):
            part = scores[:, j * HEAD : (j + 1) * HEAD]
            row_max = jnp.max(part, axis=-1, keepdims=True)
            exp_part = jnp.exp(part - row_max)
            row_total = jnp.sum(exp_part, axis=-1, keepdims=True)
            rounded = exp_part.astype(jnp.bfloat16).astype(jnp.float32)
            dotted = jnp.sum(
                rounded * grad_probs[:, j * HEAD : (j + 1) * HEAD], axis=-1, keepdims=True
            )
            maxes.append(row_max)
            totals.append(row_total)
            dots.append(dotted / row_total)
        top = maxes[0]
        for j in range(1, NBRS):
            top = jnp.maximum(top, maxes[j])
        weights = [totals[j] * jnp.exp(maxes[j] - top) for j in range(NBRS)]
        weight_sum = weights[0]
        weighted = weights[0] * dots[0]
        for j in range(1, NBRS):
            weight_sum = weight_sum + weights[j]
            weighted = weighted + weights[j] * dots[j]
        log_total = top + jnp.log(weight_sum)
        delta = weighted / weight_sum
        probs = jnp.exp(scores - log_total)
        grad_scores = (probs * (grad_probs - delta)).astype(jnp.bfloat16)
        window = jnp.zeros(query.shape, jnp.float32)
        for j in range(NBRS):
            part = lax.dot_general(
                grad_scores[:, j * HEAD : (j + 1) * HEAD],
                keys[j * HEAD : (j + 1) * HEAD],
                plain,
                preferred_element_type=jnp.float32,
            )
            window = window + (part * scale).astype(jnp.bfloat16).astype(jnp.float32)
        window_ref[span] = window.astype(window_ref.dtype)
        probs_t = probs.astype(jnp.bfloat16).astype(jnp.float32).T.astype(jnp.bfloat16)
        scores_t = grad_scores.astype(jnp.float32).T.astype(jnp.bfloat16)
        value_term = lax.dot_general(probs_t, grad, plain, preferred_element_type=jnp.float32)
        key_term = lax.dot_general(scores_t, query, plain, preferred_element_type=jnp.float32) * scale
        for j in range(NBRS):
            term_ref[span * NBRS + j, 0] = key_term[j * HEAD : (j + 1) * HEAD].astype(term_ref.dtype)
            term_ref[span * NBRS + j, 1] = value_term[j * HEAD : (j + 1) * HEAD].astype(term_ref.dtype)


def span_attention(pair_slot, window_query, window_grad, blocks):
    span_count, span_len, row_width = window_query.shape
    slot_count, _, block_len, _ = blocks.shape
    head_count = row_width // HEAD
    pair_count = span_count * NBRS

    def window_map(h, slots):
        return (0, 0, h)

    def block_map(h, slots):
        return (0, 0, 0, h)

    flops = 2 * span_len * block_len * HEAD * 9 * pair_count * head_count
    return pl.pallas_call(
        span_kernel,
        grid_spec=pltpu.PrefetchScalarGridSpec(
            num_scalar_prefetch=1,
            grid=(head_count,),
            in_specs=[
                pl.BlockSpec((span_count, span_len, HEAD), window_map),
                pl.BlockSpec((span_count, span_len, HEAD), window_map),
                pl.BlockSpec((slot_count, 2, block_len, HEAD), block_map),
            ],
            out_specs=[
                pl.BlockSpec((span_count, span_len, HEAD), window_map),
                pl.BlockSpec((pair_count, 2, block_len, HEAD), block_map),
            ],
        ),
        out_shape=[
            jax.ShapeDtypeStruct((span_count, span_len, row_width), jnp.bfloat16),
            jax.ShapeDtypeStruct((pair_count, 2, block_len, row_width), jnp.bfloat16),
        ],
        cost_estimate=pl.CostEstimate(
            flops=flops,
            transcendentals=2 * pair_count * span_len * block_len * head_count,
            bytes_accessed=2 * (2 * blocks.size + 3 * window_query.size),
        ),
    )(pair_slot, window_query, window_grad, blocks)


def gather_kernel(held_ref, out_ref, send_sem, recv_sem, local_sem):
    groups = lax.axis_size("grp")
    me = lax.axis_index("grp")
    column = lax.axis_index("seq")
    ahead = groups // 2
    behind = groups - 1 - ahead
    up = lax.rem(me + 1, groups)
    down = lax.rem(me + groups - 1, groups)
    barrier = pltpu.get_barrier_semaphore()
    for neighbour in (up, down):
        pl.semaphore_signal(
            barrier, 1, device_id=(neighbour, column), device_id_type=pl.DeviceIdType.MESH
        )
    pl.semaphore_wait(barrier, 2)
    local = pltpu.make_async_copy(held_ref, out_ref.at[0], local_sem)
    local.start()
    rows = held_ref.shape[1] // 2
    parts = [(kind, half) for kind in range(2) for half in range(2)]
    pending, started = {}, []
    for step in range(1, ahead + 1):
        for part, (kind, half) in enumerate(parts):
            span = pl.ds(half * rows, rows)
            for direction in (0, 1):
                if direction == 1 and step > behind:
                    continue
                if direction == 0:
                    source, target, device = groups + 1 - step, groups - step, up
                else:
                    source, target, device = step - 1, step, down
                if step > 1:
                    pending.pop((direction, part)).wait_recv()
                copy = pltpu.make_async_remote_copy(
                    src_ref=held_ref.at[kind, span] if step == 1 else out_ref.at[source, kind, span],
                    dst_ref=out_ref.at[target, kind, span],
                    send_sem=send_sem.at[direction, step - 1, part],
                    recv_sem=recv_sem.at[direction, step - 1, part],
                    device_id=(device, column),
                    device_id_type=pl.DeviceIdType.MESH,
                )
                copy.start()
                pending[(direction, part)] = copy
                started.append(copy)
    for copy in pending.values():
        copy.wait_recv()
    for copy in started:
        copy.wait_send()
    local.wait()


def ring_gather(held, groups):
    ahead = groups // 2
    return pl.pallas_call(
        gather_kernel,
        out_shape=jax.ShapeDtypeStruct((groups,) + held.shape, held.dtype),
        in_specs=[pl.BlockSpec(memory_space=pl.ANY)],
        out_specs=pl.BlockSpec(memory_space=pl.ANY),
        scratch_shapes=[
            pltpu.SemaphoreType.DMA((2, ahead, 4)),
            pltpu.SemaphoreType.DMA((2, ahead, 4)),
            pltpu.SemaphoreType.DMA(()),
        ],
        compiler_params=pltpu.CompilerParams(collective_id=0, has_side_effects=True),
    )(held)


def ring_step(array, axis, by):
    length = lax.axis_size(axis)
    pairs = [(i, (i + by) % length) for i in range(length)]
    return lax.ppermute(array, axis, pairs)


def shards(queries, grad_out, neighbour_keys, neighbour_values, neighbours):
    groups = lax.axis_size("grp")
    me = lax.axis_index("grp")
    span_len = SPAN
    tok_rows = queries.shape[1]
    row_width = queries.shape[2]
    head_count = row_width // HEAD
    neighbour_len = neighbour_keys.shape[2]
    span_count = tok_rows // span_len
    pair_count = span_count * NBRS
    assert pair_count == groups
    score_scale = HEAD ** (-0.5)
    ahead = groups // 2
    behind = groups - 1 - ahead
    next_query, next_grad = from_behind(
        (queries[0, : span_len - 1], grad_out[0, : span_len - 1]), "seq", -1
    )
    window_query = jnp.concatenate([queries[0, span_len - 1 :], next_query], axis=0).reshape(
        span_count, span_len, row_width
    )
    window_grad = jnp.concatenate([grad_out[0, span_len - 1 :], next_grad], axis=0).reshape(
        span_count, span_len, row_width
    )
    owner_ids = neighbours[0].reshape(pair_count)
    group_ids = jnp.arange(groups, dtype=jnp.int32)
    placement = (owner_ids[None, :] == group_ids[:, None]).astype(jnp.int32)
    rel_groups = (me + group_ids) % groups
    pair_slot = (owner_ids - me) % groups
    held = jnp.stack([neighbour_keys[0, 0], neighbour_values[0, 0]])
    all_blocks = ring_gather(held, groups)
    grad_windows, pair_terms = span_attention(pair_slot, window_query, window_grad, all_blocks)
    grad_windows = grad_windows.reshape(1, span_count, span_len, row_width)
    slot_pair = jnp.sum(placement * jnp.arange(pair_count, dtype=jnp.int32)[None, :], axis=1)
    slot_pair = slot_pair[rel_groups]

    def terms(slot):
        return lax.dynamic_index_in_dim(pair_terms, slot_pair[slot], axis=0, keepdims=False)

    up_sum = terms(ahead)
    down_sum = terms(groups - behind)
    for step in range(1, ahead + 1):
        up_arrived = ring_step(up_sum, "grp", 1).astype(jnp.float32)
        if step <= behind:
            down_arrived = ring_step(down_sum, "grp", -1).astype(jnp.float32)
            up_arrived, down_arrived = lax.optimization_barrier((up_arrived, down_arrived))
        if step < ahead:
            up_sum = (up_arrived + terms(ahead - step)).astype(jnp.bfloat16)
        if step < behind:
            down_sum = (down_arrived + terms(groups - behind + step)).astype(jnp.bfloat16)
    total = up_arrived + down_arrived + terms(0).astype(jnp.float32)
    grad_keys = total[0].astype(jnp.bfloat16).reshape(1, 1, neighbour_len, row_width)
    grad_values = total[1].astype(jnp.bfloat16).reshape(1, 1, neighbour_len, row_width)
    return (grad_windows, grad_keys, grad_values)


def solution(mesh):
    in_specs = (
        P("grp", "seq", None),
        P("grp", "seq", None),
        P("grp", "seq", None, None),
        P("grp", "seq", None, None),
        P("grp", "seq", None),
    )
    out_specs = (
        P("grp", "seq", None, None),
        P("grp", "seq", None, None),
        P("grp", "seq", None, None),
    )
    return jax.shard_map(shards, mesh=mesh, in_specs=in_specs, out_specs=out_specs, check_vma=False)
```

```python
import jax
import jax.numpy as jnp
from jax import lax
from jax.experimental import pallas as pl
from jax.experimental.pallas import tpu as pltpu
from jax.sharding import PartitionSpec as P

HEAD = 128
SPAN = 64
NBRS = 4


def from_behind(array, axis, by):
    length = lax.axis_size(axis)
    pairs = [(i, i + by) for i in range(length) if 0 <= i + by < length]
    return lax.ppermute(array, axis, pairs)


def span_kernel(slot_ref, query_ref, grad_ref, block_ref, window_ref, term_ref):
    scale = HEAD ** (-0.5)
    contract_last = (((1,), (1,)), ((), ()))
    plain = (((1,), (0,)), ((), ()))
    for span in range(query_ref.shape[0]):
        query = query_ref[span]
        grad = grad_ref[span]
        slots = [slot_ref[span * NBRS + j] for j in range(NBRS)]
        keys = jnp.concatenate([block_ref[slot, 0] for slot in slots], axis=0)
        values = jnp.concatenate([block_ref[slot, 1] for slot in slots], axis=0)
        scores = lax.dot_general(query, keys, contract_last, preferred_element_type=jnp.float32) * scale
        grad_probs = lax.dot_general(grad, values, contract_last, preferred_element_type=jnp.float32)
        maxes, totals, dots = [], [], []
        for j in range(NBRS):
            part = scores[:, j * HEAD : (j + 1) * HEAD]
            row_max = jnp.max(part, axis=-1, keepdims=True)
            exp_part = jnp.exp(part - row_max)
            row_total = jnp.sum(exp_part, axis=-1, keepdims=True)
            rounded = exp_part.astype(jnp.bfloat16).astype(jnp.float32)
            dotted = jnp.sum(
                rounded * grad_probs[:, j * HEAD : (j + 1) * HEAD], axis=-1, keepdims=True
            )
            maxes.append(row_max)
            totals.append(row_total)
            dots.append(dotted / row_total)
        top = maxes[0]
        for j in range(1, NBRS):
            top = jnp.maximum(top, maxes[j])
        weights = [totals[j] * jnp.exp(maxes[j] - top) for j in range(NBRS)]
        weight_sum = weights[0]
        weighted = weights[0] * dots[0]
        for j in range(1, NBRS):
            weight_sum = weight_sum + weights[j]
            weighted = weighted + weights[j] * dots[j]
        log_total = top + jnp.log(weight_sum)
        delta = weighted / weight_sum
        probs = jnp.exp(scores - log_total)
        grad_scores = (probs * (grad_probs - delta)).astype(jnp.bfloat16)
        window = jnp.zeros(query.shape, jnp.float32)
        for j in range(NBRS):
            part = lax.dot_general(
                grad_scores[:, j * HEAD : (j + 1) * HEAD],
                keys[j * HEAD : (j + 1) * HEAD],
                plain,
                preferred_element_type=jnp.float32,
            )
            window = window + (part * scale).astype(jnp.bfloat16).astype(jnp.float32)
        window_ref[span] = window.astype(window_ref.dtype)
        probs_t = probs.astype(jnp.bfloat16).astype(jnp.float32).T.astype(jnp.bfloat16)
        scores_t = grad_scores.astype(jnp.float32).T.astype(jnp.bfloat16)
        value_term = lax.dot_general(probs_t, grad, plain, preferred_element_type=jnp.float32)
        key_term = lax.dot_general(scores_t, query, plain, preferred_element_type=jnp.float32) * scale
        for j in range(NBRS):
            term_ref[span * NBRS + j, 0] = key_term[j * HEAD : (j + 1) * HEAD].astype(term_ref.dtype)
            term_ref[span * NBRS + j, 1] = value_term[j * HEAD : (j + 1) * HEAD].astype(term_ref.dtype)


def span_attention(pair_slot, window_query, window_grad, blocks):
    span_count, span_len, row_width = window_query.shape
    slot_count, _, block_len, _ = blocks.shape
    head_count = row_width // HEAD
    pair_count = span_count * NBRS

    def window_map(h, slots):
        return (0, 0, h)

    def block_map(h, slots):
        return (0, 0, 0, h)

    flops = 2 * span_len * block_len * HEAD * 9 * pair_count * head_count
    return pl.pallas_call(
        span_kernel,
        grid_spec=pltpu.PrefetchScalarGridSpec(
            num_scalar_prefetch=1,
            grid=(head_count,),
            in_specs=[
                pl.BlockSpec((span_count, span_len, HEAD), window_map),
                pl.BlockSpec((span_count, span_len, HEAD), window_map),
                pl.BlockSpec((slot_count, 2, block_len, HEAD), block_map),
            ],
            out_specs=[
                pl.BlockSpec((span_count, span_len, HEAD), window_map),
                pl.BlockSpec((pair_count, 2, block_len, HEAD), block_map),
            ],
        ),
        out_shape=[
            jax.ShapeDtypeStruct((span_count, span_len, row_width), jnp.bfloat16),
            jax.ShapeDtypeStruct((pair_count, 2, block_len, row_width), jnp.bfloat16),
        ],
        cost_estimate=pl.CostEstimate(
            flops=flops,
            transcendentals=2 * pair_count * span_len * block_len * head_count,
            bytes_accessed=2 * (2 * blocks.size + 3 * window_query.size),
        ),
    )(pair_slot, window_query, window_grad, blocks)


def gather_kernel(key_ref, value_ref, out_ref, send_sem, recv_sem, local_sem):
    groups = lax.axis_size("grp")
    me = lax.axis_index("grp")
    column = lax.axis_index("seq")
    ahead = groups // 2
    behind = groups - 1 - ahead
    up = lax.rem(me + 1, groups)
    down = lax.rem(me + groups - 1, groups)
    barrier = pltpu.get_barrier_semaphore()
    for neighbour in (up, down):
        pl.semaphore_signal(
            barrier, 1, device_id=(neighbour, column), device_id_type=pl.DeviceIdType.MESH
        )
    pl.semaphore_wait(barrier, 2)
    own = (key_ref.at[0, 0], value_ref.at[0, 0])
    locals_ = [
        pltpu.make_async_copy(own[kind], out_ref.at[0, kind], local_sem.at[kind]) for kind in range(2)
    ]
    for copy in locals_:
        copy.start()
    for step in range(1, ahead + 1):
        routes = [(0, groups + 1 - step, groups - step, up)]
        if step <= behind:
            routes.append((1, step - 1, step, down))
        copies = []
        for direction, source, target, device in routes:
            if step == 1:
                pieces = [(own[kind], out_ref.at[target, kind], kind) for kind in range(2)]
            else:
                pieces = [(out_ref.at[source], out_ref.at[target], 0)]
            for src, dst, part in pieces:
                copies.append(
                    pltpu.make_async_remote_copy(
                        src_ref=src,
                        dst_ref=dst,
                        send_sem=send_sem.at[direction, step - 1, part],
                        recv_sem=recv_sem.at[direction, step - 1, part],
                        device_id=(device, column),
                        device_id_type=pl.DeviceIdType.MESH,
                    )
                )
        for copy in copies:
            copy.start()
        for copy in copies:
            copy.wait()
    for copy in locals_:
        copy.wait()


def ring_gather(keys, values, groups):
    ahead = groups // 2
    block_shape = keys.shape[2:]
    return pl.pallas_call(
        gather_kernel,
        out_shape=jax.ShapeDtypeStruct((groups, 2) + block_shape, keys.dtype),
        in_specs=[pl.BlockSpec(memory_space=pl.ANY), pl.BlockSpec(memory_space=pl.ANY)],
        out_specs=pl.BlockSpec(memory_space=pl.ANY),
        scratch_shapes=[
            pltpu.SemaphoreType.DMA((2, ahead, 2)),
            pltpu.SemaphoreType.DMA((2, ahead, 2)),
            pltpu.SemaphoreType.DMA((2,)),
        ],
        compiler_params=pltpu.CompilerParams(collective_id=0, has_side_effects=True),
    )(keys, values)


def ring_step(array, axis, by):
    length = lax.axis_size(axis)
    pairs = [(i, (i + by) % length) for i in range(length)]
    return lax.ppermute(array, axis, pairs)


def shards(queries, grad_out, neighbour_keys, neighbour_values, neighbours):
    groups = lax.axis_size("grp")
    me = lax.axis_index("grp")
    span_len = SPAN
    tok_rows = queries.shape[1]
    row_width = queries.shape[2]
    head_count = row_width // HEAD
    neighbour_len = neighbour_keys.shape[2]
    span_count = tok_rows // span_len
    pair_count = span_count * NBRS
    assert pair_count == groups
    score_scale = HEAD ** (-0.5)
    ahead = groups // 2
    behind = groups - 1 - ahead
    next_query, next_grad = from_behind(
        (queries[0, : span_len - 1], grad_out[0, : span_len - 1]), "seq", -1
    )
    window_query = jnp.concatenate([queries[0, span_len - 1 :], next_query], axis=0).reshape(
        span_count, span_len, row_width
    )
    window_grad = jnp.concatenate([grad_out[0, span_len - 1 :], next_grad], axis=0).reshape(
        span_count, span_len, row_width
    )
    owner_ids = neighbours[0].reshape(pair_count)
    group_ids = jnp.arange(groups, dtype=jnp.int32)
    placement = (owner_ids[None, :] == group_ids[:, None]).astype(jnp.int32)
    rel_groups = (me + group_ids) % groups
    pair_slot = (owner_ids - me) % groups
    all_blocks = ring_gather(neighbour_keys, neighbour_values, groups)
    grad_windows, pair_terms = span_attention(pair_slot, window_query, window_grad, all_blocks)
    grad_windows = grad_windows.reshape(1, span_count, span_len, row_width)
    slot_pair = jnp.sum(placement * jnp.arange(pair_count, dtype=jnp.int32)[None, :], axis=1)
    slot_pair = slot_pair[rel_groups]

    def terms(slot):
        return lax.dynamic_index_in_dim(pair_terms, slot_pair[slot], axis=0, keepdims=False)

    up_sum = terms(ahead)
    down_sum = terms(groups - behind)
    for step in range(1, ahead + 1):
        up_arrived = ring_step(up_sum, "grp", 1).astype(jnp.float32)
        if step <= behind:
            down_arrived = ring_step(down_sum, "grp", -1).astype(jnp.float32)
            up_arrived, down_arrived = lax.optimization_barrier((up_arrived, down_arrived))
        if step < ahead:
            up_sum = (up_arrived + terms(ahead - step)).astype(jnp.bfloat16)
        if step < behind:
            down_sum = (down_arrived + terms(groups - behind + step)).astype(jnp.bfloat16)
    total = up_arrived + down_arrived + terms(0).astype(jnp.float32)
    grad_keys = total[0].astype(jnp.bfloat16).reshape(1, 1, neighbour_len, row_width)
    grad_values = total[1].astype(jnp.bfloat16).reshape(1, 1, neighbour_len, row_width)
    return (grad_windows, grad_keys, grad_values)


def solution(mesh):
    in_specs = (
        P("grp", "seq", None),
        P("grp", "seq", None),
        P("grp", "seq", None, None),
        P("grp", "seq", None, None),
        P("grp", "seq", None),
    )
    out_specs = (
        P("grp", "seq", None, None),
        P("grp", "seq", None, None),
        P("grp", "seq", None, None),
    )
    return jax.shard_map(shards, mesh=mesh, in_specs=in_specs, out_specs=out_specs, check_vma=False)
```

```python
import jax
import jax.numpy as jnp
from jax import lax
from jax.experimental import pallas as pl
from jax.experimental.pallas import tpu as pltpu
from jax.sharding import PartitionSpec as P

HEAD = 128
SPAN = 64
NBRS = 4


def from_behind(array, axis, by):
    length = lax.axis_size(axis)
    pairs = [(i, i + by) for i in range(length) if 0 <= i + by < length]
    return lax.ppermute(array, axis, pairs)


def span_kernel(slot_ref, query_ref, grad_ref, block_ref, window_ref, term_ref):
    scale = HEAD ** (-0.5)
    contract_last = (((1,), (1,)), ((), ()))
    plain = (((1,), (0,)), ((), ()))
    for span in range(query_ref.shape[0]):
        query = query_ref[span]
        grad = grad_ref[span]
        slots = [slot_ref[span * NBRS + j] for j in range(NBRS)]
        keys = jnp.concatenate([block_ref[slot, 0] for slot in slots], axis=0)
        values = jnp.concatenate([block_ref[slot, 1] for slot in slots], axis=0)
        scores = lax.dot_general(query, keys, contract_last, preferred_element_type=jnp.float32) * scale
        grad_probs = lax.dot_general(grad, values, contract_last, preferred_element_type=jnp.float32)
        maxes, totals, dots = [], [], []
        for j in range(NBRS):
            part = scores[:, j * HEAD : (j + 1) * HEAD]
            row_max = jnp.max(part, axis=-1, keepdims=True)
            exp_part = jnp.exp(part - row_max)
            row_total = jnp.sum(exp_part, axis=-1, keepdims=True)
            rounded = exp_part.astype(jnp.bfloat16).astype(jnp.float32)
            dotted = jnp.sum(
                rounded * grad_probs[:, j * HEAD : (j + 1) * HEAD], axis=-1, keepdims=True
            )
            maxes.append(row_max)
            totals.append(row_total)
            dots.append(dotted / row_total)
        top = maxes[0]
        for j in range(1, NBRS):
            top = jnp.maximum(top, maxes[j])
        weights = [totals[j] * jnp.exp(maxes[j] - top) for j in range(NBRS)]
        weight_sum = weights[0]
        weighted = weights[0] * dots[0]
        for j in range(1, NBRS):
            weight_sum = weight_sum + weights[j]
            weighted = weighted + weights[j] * dots[j]
        log_total = top + jnp.log(weight_sum)
        delta = weighted / weight_sum
        probs = jnp.exp(scores - log_total)
        grad_scores = (probs * (grad_probs - delta)).astype(jnp.bfloat16)
        window = jnp.zeros(query.shape, jnp.float32)
        for j in range(NBRS):
            part = lax.dot_general(
                grad_scores[:, j * HEAD : (j + 1) * HEAD],
                keys[j * HEAD : (j + 1) * HEAD],
                plain,
                preferred_element_type=jnp.float32,
            )
            window = window + (part * scale).astype(jnp.bfloat16).astype(jnp.float32)
        window_ref[span] = window.astype(window_ref.dtype)
        probs_t = probs.astype(jnp.bfloat16).astype(jnp.float32).T.astype(jnp.bfloat16)
        scores_t = grad_scores.astype(jnp.float32).T.astype(jnp.bfloat16)
        value_term = lax.dot_general(probs_t, grad, plain, preferred_element_type=jnp.float32)
        key_term = lax.dot_general(scores_t, query, plain, preferred_element_type=jnp.float32) * scale
        for j in range(NBRS):
            term_ref[slots[j], 0] = key_term[j * HEAD : (j + 1) * HEAD].astype(term_ref.dtype)
            term_ref[slots[j], 1] = value_term[j * HEAD : (j + 1) * HEAD].astype(term_ref.dtype)


def span_attention(pair_slot, window_query, window_grad, blocks):
    span_count, span_len, row_width = window_query.shape
    slot_count, _, block_len, _ = blocks.shape
    head_count = row_width // HEAD
    pair_count = span_count * NBRS

    def window_map(h, slots):
        return (0, 0, h)

    def block_map(h, slots):
        return (0, 0, 0, h)

    flops = 2 * span_len * block_len * HEAD * 9 * pair_count * head_count
    return pl.pallas_call(
        span_kernel,
        grid_spec=pltpu.PrefetchScalarGridSpec(
            num_scalar_prefetch=1,
            grid=(head_count,),
            in_specs=[
                pl.BlockSpec((span_count, span_len, HEAD), window_map),
                pl.BlockSpec((span_count, span_len, HEAD), window_map),
                pl.BlockSpec((slot_count, 2, block_len, HEAD), block_map),
            ],
            out_specs=[
                pl.BlockSpec((span_count, span_len, HEAD), window_map),
                pl.BlockSpec((pair_count, 2, block_len, HEAD), block_map),
            ],
        ),
        out_shape=[
            jax.ShapeDtypeStruct((span_count, span_len, row_width), jnp.bfloat16),
            jax.ShapeDtypeStruct((pair_count, 2, block_len, row_width), jnp.bfloat16),
        ],
        cost_estimate=pl.CostEstimate(
            flops=flops,
            transcendentals=2 * pair_count * span_len * block_len * head_count,
            bytes_accessed=2 * (2 * blocks.size + 3 * window_query.size),
        ),
    )(pair_slot, window_query, window_grad, blocks)


def gather_kernel(key_ref, value_ref, out_ref, send_sem, recv_sem, local_sem):
    groups = lax.axis_size("grp")
    me = lax.axis_index("grp")
    column = lax.axis_index("seq")
    ahead = groups // 2
    behind = groups - 1 - ahead
    up = lax.rem(me + 1, groups)
    down = lax.rem(me + groups - 1, groups)
    barrier = pltpu.get_barrier_semaphore()
    for neighbour in (up, down):
        pl.semaphore_signal(
            barrier, 1, device_id=(neighbour, column), device_id_type=pl.DeviceIdType.MESH
        )
    pl.semaphore_wait(barrier, 2)
    own = (key_ref.at[0, 0], value_ref.at[0, 0])
    locals_ = [
        pltpu.make_async_copy(own[kind], out_ref.at[0, kind], local_sem.at[kind]) for kind in range(2)
    ]
    for copy in locals_:
        copy.start()
    for step in range(1, ahead + 1):
        routes = [(0, groups + 1 - step, groups - step, up)]
        if step <= behind:
            routes.append((1, step - 1, step, down))
        copies = []
        for direction, source, target, device in routes:
            if step == 1:
                pieces = [(own[kind], out_ref.at[target, kind], kind) for kind in range(2)]
            else:
                pieces = [(out_ref.at[source], out_ref.at[target], 0)]
            for src, dst, part in pieces:
                copies.append(
                    pltpu.make_async_remote_copy(
                        src_ref=src,
                        dst_ref=dst,
                        send_sem=send_sem.at[direction, step - 1, part],
                        recv_sem=recv_sem.at[direction, step - 1, part],
                        device_id=(device, column),
                        device_id_type=pl.DeviceIdType.MESH,
                    )
                )
        for copy in copies:
            copy.start()
        for copy in copies:
            copy.wait()
    for copy in locals_:
        copy.wait()


def ring_gather(keys, values, groups):
    ahead = groups // 2
    block_shape = keys.shape[2:]
    return pl.pallas_call(
        gather_kernel,
        out_shape=jax.ShapeDtypeStruct((groups, 2) + block_shape, keys.dtype),
        in_specs=[pl.BlockSpec(memory_space=pl.ANY), pl.BlockSpec(memory_space=pl.ANY)],
        out_specs=pl.BlockSpec(memory_space=pl.ANY),
        scratch_shapes=[
            pltpu.SemaphoreType.DMA((2, ahead, 2)),
            pltpu.SemaphoreType.DMA((2, ahead, 2)),
            pltpu.SemaphoreType.DMA((2,)),
        ],
        compiler_params=pltpu.CompilerParams(collective_id=0, has_side_effects=True),
    )(keys, values)


def add_rows(target, first, second):
    rows = 16

    def body(index, carry):
        part = pl.ds(pl.multiple_of(index * rows, rows), rows)
        for kind in range(target.shape[0]):
            total = first[kind, part].astype(jnp.float32) + second[kind, part].astype(jnp.float32)
            target[kind, part] = total.astype(target.dtype)
        return carry

    lax.fori_loop(0, target.shape[1] // rows, body, 0)


def reduce_kernel(term_ref, out_ref, own, recv_up, recv_down, send_up, send_down, local_sem, send_sem, recv_sem):
    groups = lax.axis_size("grp")
    me = lax.axis_index("grp")
    column = lax.axis_index("seq")
    ahead = groups // 2
    behind = groups - 1 - ahead
    up = lax.rem(me + 1, groups)
    down = lax.rem(me + groups - 1, groups)
    barrier = pltpu.get_barrier_semaphore()
    for neighbour in (up, down):
        pl.semaphore_signal(
            barrier, 1, device_id=(neighbour, column), device_id_type=pl.DeviceIdType.MESH
        )
    pl.semaphore_wait(barrier, 2)
    load = pltpu.make_async_copy(term_ref, own, local_sem)
    load.start()
    for step in range(1, ahead + 1):
        if step == 2:
            load.wait()
        routes = [(0, up, recv_up, send_up, term_ref.at[ahead], ahead - step + 1)]
        if step <= behind:
            routes.append((1, down, recv_down, send_down, term_ref.at[groups - behind], groups - behind + step - 1))
        copies = []
        for direction, device, recv, send, first, slot in routes:
            if step == 1:
                source = first
            else:
                add_rows(send.at[step - 2], recv.at[step - 2], own.at[slot])
                source = send.at[step - 2]
            copies.append(
                pltpu.make_async_remote_copy(
                    src_ref=source,
                    dst_ref=recv.at[step - 1],
                    send_sem=send_sem.at[direction, step - 1],
                    recv_sem=recv_sem.at[direction, step - 1],
                    device_id=(device, column),
                    device_id_type=pl.DeviceIdType.MESH,
                )
            )
            copies[-1].start()
        for copy in copies:
            copy.wait()
    rows = 16

    def body(index, carry):
        part = pl.ds(pl.multiple_of(index * rows, rows), rows)
        for kind in range(out_ref.shape[0]):
            total = (
                recv_up[ahead - 1, kind, part].astype(jnp.float32)
                + recv_down[behind - 1, kind, part].astype(jnp.float32)
                + own[0, kind, part].astype(jnp.float32)
            )
            out_ref[kind, part] = total.astype(out_ref.dtype)
        return carry

    lax.fori_loop(0, out_ref.shape[1] // rows, body, 0)


def ring_reduce(terms, groups):
    ahead = groups // 2
    behind = groups - 1 - ahead
    block = terms.shape[1:]
    return pl.pallas_call(
        reduce_kernel,
        out_shape=jax.ShapeDtypeStruct(block, terms.dtype),
        in_specs=[pl.BlockSpec(memory_space=pl.ANY)],
        out_specs=pl.BlockSpec(memory_space=pltpu.VMEM),
        scratch_shapes=[
            pltpu.VMEM(terms.shape, terms.dtype),
            pltpu.VMEM((ahead,) + block, terms.dtype),
            pltpu.VMEM((behind,) + block, terms.dtype),
            pltpu.VMEM((ahead - 1,) + block, terms.dtype),
            pltpu.VMEM((behind - 1,) + block, terms.dtype),
            pltpu.SemaphoreType.DMA(()),
            pltpu.SemaphoreType.DMA((2, ahead)),
            pltpu.SemaphoreType.DMA((2, ahead)),
        ],
        compiler_params=pltpu.CompilerParams(
            collective_id=1, has_side_effects=True, vmem_limit_bytes=60 * 1024 * 1024
        ),
    )(terms)


def ring_step(array, axis, by):
    length = lax.axis_size(axis)
    pairs = [(i, (i + by) % length) for i in range(length)]
    return lax.ppermute(array, axis, pairs)


def shards(queries, grad_out, neighbour_keys, neighbour_values, neighbours):
    groups = lax.axis_size("grp")
    me = lax.axis_index("grp")
    span_len = SPAN
    tok_rows = queries.shape[1]
    row_width = queries.shape[2]
    head_count = row_width // HEAD
    neighbour_len = neighbour_keys.shape[2]
    span_count = tok_rows // span_len
    pair_count = span_count * NBRS
    assert pair_count == groups
    score_scale = HEAD ** (-0.5)
    ahead = groups // 2
    behind = groups - 1 - ahead
    next_query, next_grad = from_behind(
        (queries[0, : span_len - 1], grad_out[0, : span_len - 1]), "seq", -1
    )
    window_query = jnp.concatenate([queries[0, span_len - 1 :], next_query], axis=0).reshape(
        span_count, span_len, row_width
    )
    window_grad = jnp.concatenate([grad_out[0, span_len - 1 :], next_grad], axis=0).reshape(
        span_count, span_len, row_width
    )
    owner_ids = neighbours[0].reshape(pair_count)
    group_ids = jnp.arange(groups, dtype=jnp.int32)
    placement = (owner_ids[None, :] == group_ids[:, None]).astype(jnp.int32)
    rel_groups = (me + group_ids) % groups
    pair_slot = (owner_ids - me) % groups
    all_blocks = ring_gather(neighbour_keys, neighbour_values, groups)
    grad_windows, pair_terms = span_attention(pair_slot, window_query, window_grad, all_blocks)
    grad_windows = grad_windows.reshape(1, span_count, span_len, row_width)
    total = ring_reduce(pair_terms, groups)
    grad_keys = total[0].astype(jnp.bfloat16).reshape(1, 1, neighbour_len, row_width)
    grad_values = total[1].astype(jnp.bfloat16).reshape(1, 1, neighbour_len, row_width)
    return (grad_windows, grad_keys, grad_values)


def solution(mesh):
    in_specs = (
        P("grp", "seq", None),
        P("grp", "seq", None),
        P("grp", "seq", None, None),
        P("grp", "seq", None, None),
        P("grp", "seq", None),
    )
    out_specs = (
        P("grp", "seq", None, None),
        P("grp", "seq", None, None),
        P("grp", "seq", None, None),
    )
    return jax.shard_map(shards, mesh=mesh, in_specs=in_specs, out_specs=out_specs, check_vma=False)
```

```python
import jax
import jax.numpy as jnp
from jax import lax
from jax.experimental import pallas as pl
from jax.experimental.pallas import tpu as pltpu
from jax.sharding import PartitionSpec as P

HEAD = 128
SPAN = 64
NBRS = 4


def from_behind(array, axis, by):
    length = lax.axis_size(axis)
    pairs = [(i, i + by) for i in range(length) if 0 <= i + by < length]
    return lax.ppermute(array, axis, pairs)


def span_kernel(slot_ref, query_ref, grad_ref, block_ref, window_ref, term_ref):
    scale = HEAD ** (-0.5)
    contract_last = (((1,), (1,)), ((), ()))
    plain = (((1,), (0,)), ((), ()))
    for span in range(query_ref.shape[0]):
        query = query_ref[span]
        grad = grad_ref[span]
        slots = [slot_ref[span * NBRS + j] for j in range(NBRS)]
        keys = jnp.concatenate([block_ref[slot, 0] for slot in slots], axis=0)
        values = jnp.concatenate([block_ref[slot, 1] for slot in slots], axis=0)
        scores = lax.dot_general(query, keys, contract_last, preferred_element_type=jnp.float32) * scale
        grad_probs = lax.dot_general(grad, values, contract_last, preferred_element_type=jnp.float32)
        maxes, totals, dots = [], [], []
        for j in range(NBRS):
            part = scores[:, j * HEAD : (j + 1) * HEAD]
            row_max = jnp.max(part, axis=-1, keepdims=True)
            exp_part = jnp.exp(part - row_max)
            row_total = jnp.sum(exp_part, axis=-1, keepdims=True)
            rounded = exp_part.astype(jnp.bfloat16).astype(jnp.float32)
            dotted = jnp.sum(
                rounded * grad_probs[:, j * HEAD : (j + 1) * HEAD], axis=-1, keepdims=True
            )
            maxes.append(row_max)
            totals.append(row_total)
            dots.append(dotted / row_total)
        top = maxes[0]
        for j in range(1, NBRS):
            top = jnp.maximum(top, maxes[j])
        weights = [totals[j] * jnp.exp(maxes[j] - top) for j in range(NBRS)]
        weight_sum = weights[0]
        weighted = weights[0] * dots[0]
        for j in range(1, NBRS):
            weight_sum = weight_sum + weights[j]
            weighted = weighted + weights[j] * dots[j]
        log_total = top + jnp.log(weight_sum)
        delta = weighted / weight_sum
        probs = jnp.exp(scores - log_total)
        grad_scores = (probs * (grad_probs - delta)).astype(jnp.bfloat16)
        window = jnp.zeros(query.shape, jnp.float32)
        for j in range(NBRS):
            part = lax.dot_general(
                grad_scores[:, j * HEAD : (j + 1) * HEAD],
                keys[j * HEAD : (j + 1) * HEAD],
                plain,
                preferred_element_type=jnp.float32,
            )
            window = window + (part * scale).astype(jnp.bfloat16).astype(jnp.float32)
        window_ref[span] = window.astype(window_ref.dtype)
        probs_t = probs.astype(jnp.bfloat16).astype(jnp.float32).T.astype(jnp.bfloat16)
        scores_t = grad_scores.astype(jnp.float32).T.astype(jnp.bfloat16)
        value_term = lax.dot_general(probs_t, grad, plain, preferred_element_type=jnp.float32)
        key_term = lax.dot_general(scores_t, query, plain, preferred_element_type=jnp.float32) * scale
        for j in range(NBRS):
            term_ref[slots[j], 0] = key_term[j * HEAD : (j + 1) * HEAD].astype(term_ref.dtype)
            term_ref[slots[j], 1] = value_term[j * HEAD : (j + 1) * HEAD].astype(term_ref.dtype)


def span_attention(pair_slot, window_query, window_grad, blocks):
    span_count, span_len, row_width = window_query.shape
    slot_count, _, block_len, _ = blocks.shape
    head_count = row_width // HEAD
    pair_count = span_count * NBRS

    def window_map(h, slots):
        return (0, 0, h)

    def block_map(h, slots):
        return (0, 0, 0, h)

    flops = 2 * span_len * block_len * HEAD * 9 * pair_count * head_count
    return pl.pallas_call(
        span_kernel,
        grid_spec=pltpu.PrefetchScalarGridSpec(
            num_scalar_prefetch=1,
            grid=(head_count,),
            in_specs=[
                pl.BlockSpec((span_count, span_len, HEAD), window_map),
                pl.BlockSpec((span_count, span_len, HEAD), window_map),
                pl.BlockSpec((slot_count, 2, block_len, HEAD), block_map),
            ],
            out_specs=[
                pl.BlockSpec((span_count, span_len, HEAD), window_map),
                pl.BlockSpec((pair_count, 2, block_len, HEAD), block_map),
            ],
        ),
        out_shape=[
            jax.ShapeDtypeStruct((span_count, span_len, row_width), jnp.bfloat16),
            jax.ShapeDtypeStruct((pair_count, 2, block_len, row_width), jnp.bfloat16),
        ],
        cost_estimate=pl.CostEstimate(
            flops=flops,
            transcendentals=2 * pair_count * span_len * block_len * head_count,
            bytes_accessed=2 * (2 * blocks.size + 3 * window_query.size),
        ),
    )(pair_slot, window_query, window_grad, blocks)


def gather_kernel(key_ref, value_ref, out_ref, send_sem, recv_sem, local_sem):
    groups = lax.axis_size("grp")
    me = lax.axis_index("grp")
    column = lax.axis_index("seq")
    ahead = groups // 2
    behind = groups - 1 - ahead
    up = lax.rem(me + 1, groups)
    down = lax.rem(me + groups - 1, groups)
    barrier = pltpu.get_barrier_semaphore()
    for neighbour in (up, down):
        pl.semaphore_signal(
            barrier, 1, device_id=(neighbour, column), device_id_type=pl.DeviceIdType.MESH
        )
    pl.semaphore_wait(barrier, 2)
    own = (key_ref.at[0, 0], value_ref.at[0, 0])
    locals_ = [
        pltpu.make_async_copy(own[kind], out_ref.at[0, kind], local_sem.at[kind]) for kind in range(2)
    ]
    for copy in locals_:
        copy.start()
    rows = key_ref.shape[2] // 2
    parts = [(kind, half) for kind in range(2) for half in range(2)]
    pending, started = {}, []
    for step in range(1, ahead + 1):
        for part, (kind, half) in enumerate(parts):
            span = pl.ds(half * rows, rows)
            for direction in (0, 1):
                if direction == 1 and step > behind:
                    continue
                if direction == 0:
                    source, target, device = groups + 1 - step, groups - step, up
                else:
                    source, target, device = step - 1, step, down
                if step > 1:
                    pending.pop((direction, part)).wait_recv()
                copy = pltpu.make_async_remote_copy(
                    src_ref=own[kind].at[span] if step == 1 else out_ref.at[source, kind, span],
                    dst_ref=out_ref.at[target, kind, span],
                    send_sem=send_sem.at[direction, step - 1, part],
                    recv_sem=recv_sem.at[direction, step - 1, part],
                    device_id=(device, column),
                    device_id_type=pl.DeviceIdType.MESH,
                )
                copy.start()
                pending[(direction, part)] = copy
                started.append(copy)
    for copy in pending.values():
        copy.wait_recv()
    for copy in started:
        copy.wait_send()
    for copy in locals_:
        copy.wait()


def ring_gather(keys, values, groups):
    ahead = groups // 2
    block_shape = keys.shape[2:]
    return pl.pallas_call(
        gather_kernel,
        out_shape=jax.ShapeDtypeStruct((groups, 2) + block_shape, keys.dtype),
        in_specs=[pl.BlockSpec(memory_space=pl.ANY), pl.BlockSpec(memory_space=pl.ANY)],
        out_specs=pl.BlockSpec(memory_space=pl.ANY),
        scratch_shapes=[
            pltpu.SemaphoreType.DMA((2, ahead, 4)),
            pltpu.SemaphoreType.DMA((2, ahead, 4)),
            pltpu.SemaphoreType.DMA((2,)),
        ],
        compiler_params=pltpu.CompilerParams(collective_id=0, has_side_effects=True),
    )(keys, values)


def add_rows(target, first, second):
    rows = 16

    def body(index, carry):
        part = pl.ds(pl.multiple_of(index * rows, rows), rows)
        for kind in range(target.shape[0]):
            total = first[kind, part].astype(jnp.float32) + second[kind, part].astype(jnp.float32)
            target[kind, part] = total.astype(target.dtype)
        return carry

    lax.fori_loop(0, target.shape[1] // rows, body, 0)


def reduce_kernel(term_ref, out_ref, own, recv_up, recv_down, send_up, send_down, local_sem, send_sem, recv_sem):
    groups = lax.axis_size("grp")
    me = lax.axis_index("grp")
    column = lax.axis_index("seq")
    ahead = groups // 2
    behind = groups - 1 - ahead
    up = lax.rem(me + 1, groups)
    down = lax.rem(me + groups - 1, groups)
    barrier = pltpu.get_barrier_semaphore()
    for neighbour in (up, down):
        pl.semaphore_signal(
            barrier, 1, device_id=(neighbour, column), device_id_type=pl.DeviceIdType.MESH
        )
    pl.semaphore_wait(barrier, 2)
    load = pltpu.make_async_copy(term_ref, own, local_sem)
    load.start()
    for step in range(1, ahead + 1):
        if step == 2:
            load.wait()
        routes = [(0, up, recv_up, send_up, term_ref.at[ahead], ahead - step + 1)]
        if step <= behind:
            routes.append((1, down, recv_down, send_down, term_ref.at[groups - behind], groups - behind + step - 1))
        copies = []
        for direction, device, recv, send, first, slot in routes:
            if step == 1:
                source = first
            else:
                add_rows(send.at[step - 2], recv.at[step - 2], own.at[slot])
                source = send.at[step - 2]
            copies.append(
                pltpu.make_async_remote_copy(
                    src_ref=source,
                    dst_ref=recv.at[step - 1],
                    send_sem=send_sem.at[direction, step - 1],
                    recv_sem=recv_sem.at[direction, step - 1],
                    device_id=(device, column),
                    device_id_type=pl.DeviceIdType.MESH,
                )
            )
            copies[-1].start()
        for copy in copies:
            copy.wait()
    rows = 16

    def body(index, carry):
        part = pl.ds(pl.multiple_of(index * rows, rows), rows)
        for kind in range(out_ref.shape[0]):
            total = (
                recv_up[ahead - 1, kind, part].astype(jnp.float32)
                + recv_down[behind - 1, kind, part].astype(jnp.float32)
                + own[0, kind, part].astype(jnp.float32)
            )
            out_ref[kind, part] = total.astype(out_ref.dtype)
        return carry

    lax.fori_loop(0, out_ref.shape[1] // rows, body, 0)


def ring_reduce(terms, groups):
    ahead = groups // 2
    behind = groups - 1 - ahead
    block = terms.shape[1:]
    return pl.pallas_call(
        reduce_kernel,
        out_shape=jax.ShapeDtypeStruct(block, terms.dtype),
        in_specs=[pl.BlockSpec(memory_space=pl.ANY)],
        out_specs=pl.BlockSpec(memory_space=pltpu.VMEM),
        scratch_shapes=[
            pltpu.VMEM(terms.shape, terms.dtype),
            pltpu.VMEM((ahead,) + block, terms.dtype),
            pltpu.VMEM((behind,) + block, terms.dtype),
            pltpu.VMEM((ahead - 1,) + block, terms.dtype),
            pltpu.VMEM((behind - 1,) + block, terms.dtype),
            pltpu.SemaphoreType.DMA(()),
            pltpu.SemaphoreType.DMA((2, ahead)),
            pltpu.SemaphoreType.DMA((2, ahead)),
        ],
        compiler_params=pltpu.CompilerParams(
            collective_id=1, has_side_effects=True, vmem_limit_bytes=60 * 1024 * 1024
        ),
    )(terms)


def ring_step(array, axis, by):
    length = lax.axis_size(axis)
    pairs = [(i, (i + by) % length) for i in range(length)]
    return lax.ppermute(array, axis, pairs)


def shards(queries, grad_out, neighbour_keys, neighbour_values, neighbours):
    groups = lax.axis_size("grp")
    me = lax.axis_index("grp")
    span_len = SPAN
    tok_rows = queries.shape[1]
    row_width = queries.shape[2]
    head_count = row_width // HEAD
    neighbour_len = neighbour_keys.shape[2]
    span_count = tok_rows // span_len
    pair_count = span_count * NBRS
    assert pair_count == groups
    score_scale = HEAD ** (-0.5)
    ahead = groups // 2
    behind = groups - 1 - ahead
    next_query, next_grad = from_behind(
        (queries[0, : span_len - 1], grad_out[0, : span_len - 1]), "seq", -1
    )
    window_query = jnp.concatenate([queries[0, span_len - 1 :], next_query], axis=0).reshape(
        span_count, span_len, row_width
    )
    window_grad = jnp.concatenate([grad_out[0, span_len - 1 :], next_grad], axis=0).reshape(
        span_count, span_len, row_width
    )
    owner_ids = neighbours[0].reshape(pair_count)
    group_ids = jnp.arange(groups, dtype=jnp.int32)
    placement = (owner_ids[None, :] == group_ids[:, None]).astype(jnp.int32)
    rel_groups = (me + group_ids) % groups
    pair_slot = (owner_ids - me) % groups
    all_blocks = ring_gather(neighbour_keys, neighbour_values, groups)
    grad_windows, pair_terms = span_attention(pair_slot, window_query, window_grad, all_blocks)
    grad_windows = grad_windows.reshape(1, span_count, span_len, row_width)
    total = ring_reduce(pair_terms, groups)
    grad_keys = total[0].astype(jnp.bfloat16).reshape(1, 1, neighbour_len, row_width)
    grad_values = total[1].astype(jnp.bfloat16).reshape(1, 1, neighbour_len, row_width)
    return (grad_windows, grad_keys, grad_values)


def solution(mesh):
    in_specs = (
        P("grp", "seq", None),
        P("grp", "seq", None),
        P("grp", "seq", None, None),
        P("grp", "seq", None, None),
        P("grp", "seq", None),
    )
    out_specs = (
        P("grp", "seq", None, None),
        P("grp", "seq", None, None),
        P("grp", "seq", None, None),
    )
    return jax.shard_map(shards, mesh=mesh, in_specs=in_specs, out_specs=out_specs, check_vma=False)
```

```python
import jax
import jax.numpy as jnp
from jax import lax
from jax.experimental import pallas as pl
from jax.experimental.pallas import tpu as pltpu
from jax.sharding import PartitionSpec as P

HEAD = 128
SPAN = 64
NBRS = 4


def from_behind(array, axis, by):
    length = lax.axis_size(axis)
    pairs = [(i, i + by) for i in range(length) if 0 <= i + by < length]
    return lax.ppermute(array, axis, pairs)


def span_kernel(slot_ref, query_ref, grad_ref, block_ref, window_ref, term_ref):
    scale = HEAD ** (-0.5)
    contract_last = (((1,), (1,)), ((), ()))
    plain = (((1,), (0,)), ((), ()))
    for span in range(query_ref.shape[0]):
        query = query_ref[span]
        grad = grad_ref[span]
        slots = [slot_ref[span * NBRS + j] for j in range(NBRS)]
        keys = jnp.concatenate([block_ref[slot, 0] for slot in slots], axis=0)
        values = jnp.concatenate([block_ref[slot, 1] for slot in slots], axis=0)
        scores = lax.dot_general(query, keys, contract_last, preferred_element_type=jnp.float32) * scale
        grad_probs = lax.dot_general(grad, values, contract_last, preferred_element_type=jnp.float32)
        maxes, totals, dots = [], [], []
        for j in range(NBRS):
            part = scores[:, j * HEAD : (j + 1) * HEAD]
            row_max = jnp.max(part, axis=-1, keepdims=True)
            exp_part = jnp.exp(part - row_max)
            row_total = jnp.sum(exp_part, axis=-1, keepdims=True)
            rounded = exp_part.astype(jnp.bfloat16).astype(jnp.float32)
            dotted = jnp.sum(
                rounded * grad_probs[:, j * HEAD : (j + 1) * HEAD], axis=-1, keepdims=True
            )
            maxes.append(row_max)
            totals.append(row_total)
            dots.append(dotted / row_total)
        top = maxes[0]
        for j in range(1, NBRS):
            top = jnp.maximum(top, maxes[j])
        weights = [totals[j] * jnp.exp(maxes[j] - top) for j in range(NBRS)]
        weight_sum = weights[0]
        weighted = weights[0] * dots[0]
        for j in range(1, NBRS):
            weight_sum = weight_sum + weights[j]
            weighted = weighted + weights[j] * dots[j]
        log_total = top + jnp.log(weight_sum)
        delta = weighted / weight_sum
        probs = jnp.exp(scores - log_total)
        grad_scores = (probs * (grad_probs - delta)).astype(jnp.bfloat16)
        window = jnp.zeros(query.shape, jnp.float32)
        for j in range(NBRS):
            part = lax.dot_general(
                grad_scores[:, j * HEAD : (j + 1) * HEAD],
                keys[j * HEAD : (j + 1) * HEAD],
                plain,
                preferred_element_type=jnp.float32,
            )
            window = window + (part * scale).astype(jnp.bfloat16).astype(jnp.float32)
        window_ref[span] = window.astype(window_ref.dtype)
        contract_first = (((0,), (0,)), ((), ()))
        value_term = lax.dot_general(
            probs.astype(jnp.bfloat16), grad, contract_first, preferred_element_type=jnp.float32
        )
        key_term = (
            lax.dot_general(grad_scores, query, contract_first, preferred_element_type=jnp.float32)
            * scale
        )
        for j in range(NBRS):
            term_ref[slots[j], 0] = key_term[j * HEAD : (j + 1) * HEAD].astype(term_ref.dtype)
            term_ref[slots[j], 1] = value_term[j * HEAD : (j + 1) * HEAD].astype(term_ref.dtype)


def span_attention(pair_slot, window_query, window_grad, blocks):
    span_count, span_len, row_width = window_query.shape
    slot_count, _, block_len, _ = blocks.shape
    head_count = row_width // HEAD
    pair_count = span_count * NBRS

    def window_map(h, slots):
        return (0, 0, h)

    def block_map(h, slots):
        return (0, 0, 0, h)

    flops = 2 * span_len * block_len * HEAD * 9 * pair_count * head_count
    return pl.pallas_call(
        span_kernel,
        grid_spec=pltpu.PrefetchScalarGridSpec(
            num_scalar_prefetch=1,
            grid=(head_count,),
            in_specs=[
                pl.BlockSpec((span_count, span_len, HEAD), window_map),
                pl.BlockSpec((span_count, span_len, HEAD), window_map),
                pl.BlockSpec((slot_count, 2, block_len, HEAD), block_map),
            ],
            out_specs=[
                pl.BlockSpec((span_count, span_len, HEAD), window_map),
                pl.BlockSpec((pair_count, 2, block_len, HEAD), block_map),
            ],
        ),
        out_shape=[
            jax.ShapeDtypeStruct((span_count, span_len, row_width), jnp.bfloat16),
            jax.ShapeDtypeStruct((pair_count, 2, block_len, row_width), jnp.bfloat16),
        ],
        cost_estimate=pl.CostEstimate(
            flops=flops,
            transcendentals=2 * pair_count * span_len * block_len * head_count,
            bytes_accessed=2 * (2 * blocks.size + 3 * window_query.size),
        ),
    )(pair_slot, window_query, window_grad, blocks)


def gather_kernel(key_ref, value_ref, out_ref, send_sem, recv_sem, local_sem):
    groups = lax.axis_size("grp")
    me = lax.axis_index("grp")
    column = lax.axis_index("seq")
    ahead = groups // 2
    behind = groups - 1 - ahead
    up = lax.rem(me + 1, groups)
    down = lax.rem(me + groups - 1, groups)
    barrier = pltpu.get_barrier_semaphore()
    for neighbour in (up, down):
        pl.semaphore_signal(
            barrier, 1, device_id=(neighbour, column), device_id_type=pl.DeviceIdType.MESH
        )
    pl.semaphore_wait(barrier, 2)
    own = (key_ref.at[0, 0], value_ref.at[0, 0])
    locals_ = [
        pltpu.make_async_copy(own[kind], out_ref.at[0, kind], local_sem.at[kind]) for kind in range(2)
    ]
    for copy in locals_:
        copy.start()
    for step in range(1, ahead + 1):
        routes = [(0, groups + 1 - step, groups - step, up)]
        if step <= behind:
            routes.append((1, step - 1, step, down))
        copies = []
        for direction, source, target, device in routes:
            if step == 1:
                pieces = [(own[kind], out_ref.at[target, kind], kind) for kind in range(2)]
            else:
                pieces = [(out_ref.at[source], out_ref.at[target], 0)]
            for src, dst, part in pieces:
                copies.append(
                    pltpu.make_async_remote_copy(
                        src_ref=src,
                        dst_ref=dst,
                        send_sem=send_sem.at[direction, step - 1, part],
                        recv_sem=recv_sem.at[direction, step - 1, part],
                        device_id=(device, column),
                        device_id_type=pl.DeviceIdType.MESH,
                    )
                )
        for copy in copies:
            copy.start()
        for copy in copies:
            copy.wait()
    for copy in locals_:
        copy.wait()


def ring_gather(keys, values, groups):
    ahead = groups // 2
    block_shape = keys.shape[2:]
    return pl.pallas_call(
        gather_kernel,
        out_shape=jax.ShapeDtypeStruct((groups, 2) + block_shape, keys.dtype),
        in_specs=[pl.BlockSpec(memory_space=pl.ANY), pl.BlockSpec(memory_space=pl.ANY)],
        out_specs=pl.BlockSpec(memory_space=pl.ANY),
        scratch_shapes=[
            pltpu.SemaphoreType.DMA((2, ahead, 2)),
            pltpu.SemaphoreType.DMA((2, ahead, 2)),
            pltpu.SemaphoreType.DMA((2,)),
        ],
        compiler_params=pltpu.CompilerParams(collective_id=0, has_side_effects=True),
    )(keys, values)


def add_rows(target, first, second):
    rows = 16

    def body(index, carry):
        part = pl.ds(pl.multiple_of(index * rows, rows), rows)
        for kind in range(target.shape[0]):
            total = first[kind, part].astype(jnp.float32) + second[kind, part].astype(jnp.float32)
            target[kind, part] = total.astype(target.dtype)
        return carry

    lax.fori_loop(0, target.shape[1] // rows, body, 0)


def reduce_kernel(term_ref, out_ref, own, recv_up, recv_down, send_up, send_down, local_sem, send_sem, recv_sem):
    groups = lax.axis_size("grp")
    me = lax.axis_index("grp")
    column = lax.axis_index("seq")
    ahead = groups // 2
    behind = groups - 1 - ahead
    up = lax.rem(me + 1, groups)
    down = lax.rem(me + groups - 1, groups)
    barrier = pltpu.get_barrier_semaphore()
    for neighbour in (up, down):
        pl.semaphore_signal(
            barrier, 1, device_id=(neighbour, column), device_id_type=pl.DeviceIdType.MESH
        )
    pl.semaphore_wait(barrier, 2)
    load = pltpu.make_async_copy(term_ref, own, local_sem)
    load.start()
    for step in range(1, ahead + 1):
        if step == 2:
            load.wait()
        routes = [(0, up, recv_up, send_up, term_ref.at[ahead], ahead - step + 1)]
        if step <= behind:
            routes.append((1, down, recv_down, send_down, term_ref.at[groups - behind], groups - behind + step - 1))
        copies = []
        for direction, device, recv, send, first, slot in routes:
            if step == 1:
                source = first
            else:
                add_rows(send.at[step - 2], recv.at[step - 2], own.at[slot])
                source = send.at[step - 2]
            copies.append(
                pltpu.make_async_remote_copy(
                    src_ref=source,
                    dst_ref=recv.at[step - 1],
                    send_sem=send_sem.at[direction, step - 1],
                    recv_sem=recv_sem.at[direction, step - 1],
                    device_id=(device, column),
                    device_id_type=pl.DeviceIdType.MESH,
                )
            )
            copies[-1].start()
        for copy in copies:
            copy.wait()
    rows = 16

    def body(index, carry):
        part = pl.ds(pl.multiple_of(index * rows, rows), rows)
        for kind in range(out_ref.shape[0]):
            total = (
                recv_up[ahead - 1, kind, part].astype(jnp.float32)
                + recv_down[behind - 1, kind, part].astype(jnp.float32)
                + own[0, kind, part].astype(jnp.float32)
            )
            out_ref[kind, part] = total.astype(out_ref.dtype)
        return carry

    lax.fori_loop(0, out_ref.shape[1] // rows, body, 0)


def ring_reduce(terms, groups):
    ahead = groups // 2
    behind = groups - 1 - ahead
    block = terms.shape[1:]
    return pl.pallas_call(
        reduce_kernel,
        out_shape=jax.ShapeDtypeStruct(block, terms.dtype),
        in_specs=[pl.BlockSpec(memory_space=pl.ANY)],
        out_specs=pl.BlockSpec(memory_space=pltpu.VMEM),
        scratch_shapes=[
            pltpu.VMEM(terms.shape, terms.dtype),
            pltpu.VMEM((ahead,) + block, terms.dtype),
            pltpu.VMEM((behind,) + block, terms.dtype),
            pltpu.VMEM((ahead - 1,) + block, terms.dtype),
            pltpu.VMEM((behind - 1,) + block, terms.dtype),
            pltpu.SemaphoreType.DMA(()),
            pltpu.SemaphoreType.DMA((2, ahead)),
            pltpu.SemaphoreType.DMA((2, ahead)),
        ],
        compiler_params=pltpu.CompilerParams(
            collective_id=1, has_side_effects=True, vmem_limit_bytes=60 * 1024 * 1024
        ),
    )(terms)


def ring_step(array, axis, by):
    length = lax.axis_size(axis)
    pairs = [(i, (i + by) % length) for i in range(length)]
    return lax.ppermute(array, axis, pairs)


def shards(queries, grad_out, neighbour_keys, neighbour_values, neighbours):
    groups = lax.axis_size("grp")
    me = lax.axis_index("grp")
    span_len = SPAN
    tok_rows = queries.shape[1]
    row_width = queries.shape[2]
    head_count = row_width // HEAD
    neighbour_len = neighbour_keys.shape[2]
    span_count = tok_rows // span_len
    pair_count = span_count * NBRS
    assert pair_count == groups
    score_scale = HEAD ** (-0.5)
    ahead = groups // 2
    behind = groups - 1 - ahead
    next_query, next_grad = from_behind(
        (queries[0, : span_len - 1], grad_out[0, : span_len - 1]), "seq", -1
    )
    window_query = jnp.concatenate([queries[0, span_len - 1 :], next_query], axis=0).reshape(
        span_count, span_len, row_width
    )
    window_grad = jnp.concatenate([grad_out[0, span_len - 1 :], next_grad], axis=0).reshape(
        span_count, span_len, row_width
    )
    owner_ids = neighbours[0].reshape(pair_count)
    group_ids = jnp.arange(groups, dtype=jnp.int32)
    placement = (owner_ids[None, :] == group_ids[:, None]).astype(jnp.int32)
    rel_groups = (me + group_ids) % groups
    pair_slot = (owner_ids - me) % groups
    all_blocks = ring_gather(neighbour_keys, neighbour_values, groups)
    grad_windows, pair_terms = span_attention(pair_slot, window_query, window_grad, all_blocks)
    grad_windows = grad_windows.reshape(1, span_count, span_len, row_width)
    total = ring_reduce(pair_terms, groups)
    grad_keys = total[0].astype(jnp.bfloat16).reshape(1, 1, neighbour_len, row_width)
    grad_values = total[1].astype(jnp.bfloat16).reshape(1, 1, neighbour_len, row_width)
    return (grad_windows, grad_keys, grad_values)


def solution(mesh):
    in_specs = (
        P("grp", "seq", None),
        P("grp", "seq", None),
        P("grp", "seq", None, None),
        P("grp", "seq", None, None),
        P("grp", "seq", None),
    )
    out_specs = (
        P("grp", "seq", None, None),
        P("grp", "seq", None, None),
        P("grp", "seq", None, None),
    )
    return jax.shard_map(shards, mesh=mesh, in_specs=in_specs, out_specs=out_specs, check_vma=False)
```

```python
import jax
import jax.numpy as jnp
from jax import lax
from jax.experimental import pallas as pl
from jax.experimental.pallas import tpu as pltpu
from jax.sharding import PartitionSpec as P

HEAD = 128
SPAN = 64
NBRS = 4


def from_behind(array, axis, by):
    length = lax.axis_size(axis)
    pairs = [(i, i + by) for i in range(length) if 0 <= i + by < length]
    return lax.ppermute(array, axis, pairs)


def span_kernel(slot_ref, query_ref, grad_ref, block_ref, window_ref, term_ref):
    scale = HEAD ** (-0.5)
    contract_last = (((1,), (1,)), ((), ()))
    plain = (((1,), (0,)), ((), ()))
    for span in range(query_ref.shape[0]):
        query = query_ref[span]
        grad = grad_ref[span]
        slots = [slot_ref[span * NBRS + j] for j in range(NBRS)]
        keys = jnp.concatenate([block_ref[slot, 0] for slot in slots], axis=0)
        values = jnp.concatenate([block_ref[slot, 1] for slot in slots], axis=0)
        scores = lax.dot_general(query, keys, contract_last, preferred_element_type=jnp.float32) * scale
        grad_probs = lax.dot_general(grad, values, contract_last, preferred_element_type=jnp.float32)
        maxes, totals, dots = [], [], []
        for j in range(NBRS):
            part = scores[:, j * HEAD : (j + 1) * HEAD]
            row_max = jnp.max(part, axis=-1, keepdims=True)
            exp_part = jnp.exp(part - row_max)
            row_total = jnp.sum(exp_part, axis=-1, keepdims=True)
            rounded = exp_part.astype(jnp.bfloat16).astype(jnp.float32)
            dotted = jnp.sum(
                rounded * grad_probs[:, j * HEAD : (j + 1) * HEAD], axis=-1, keepdims=True
            )
            maxes.append(row_max)
            totals.append(row_total)
            dots.append(dotted / row_total)
        top = maxes[0]
        for j in range(1, NBRS):
            top = jnp.maximum(top, maxes[j])
        weights = [totals[j] * jnp.exp(maxes[j] - top) for j in range(NBRS)]
        weight_sum = weights[0]
        weighted = weights[0] * dots[0]
        for j in range(1, NBRS):
            weight_sum = weight_sum + weights[j]
            weighted = weighted + weights[j] * dots[j]
        log_total = top + jnp.log(weight_sum)
        delta = weighted / weight_sum
        probs = jnp.exp(scores - log_total)
        grad_scores = (probs * (grad_probs - delta)).astype(jnp.bfloat16)
        window = jnp.zeros(query.shape, jnp.float32)
        for j in range(NBRS):
            part = lax.dot_general(
                grad_scores[:, j * HEAD : (j + 1) * HEAD],
                keys[j * HEAD : (j + 1) * HEAD],
                plain,
                preferred_element_type=jnp.float32,
            )
            window = window + (part * scale).astype(jnp.bfloat16).astype(jnp.float32)
        window_ref[span] = window.astype(window_ref.dtype)
        contract_first = (((0,), (0,)), ((), ()))
        value_term = lax.dot_general(
            probs.astype(jnp.bfloat16), grad, contract_first, preferred_element_type=jnp.float32
        )
        key_term = (
            lax.dot_general(grad_scores, query, contract_first, preferred_element_type=jnp.float32)
            * scale
        )
        for j in range(NBRS):
            term_ref[slots[j], 0] = key_term[j * HEAD : (j + 1) * HEAD].astype(term_ref.dtype)
            term_ref[slots[j], 1] = value_term[j * HEAD : (j + 1) * HEAD].astype(term_ref.dtype)


def span_attention(pair_slot, window_query, window_grad, blocks):
    span_count, span_len, row_width = window_query.shape
    slot_count, _, block_len, _ = blocks.shape
    head_count = row_width // HEAD
    pair_count = span_count * NBRS

    def window_map(h, slots):
        return (0, 0, h)

    def block_map(h, slots):
        return (0, 0, 0, h)

    flops = 2 * span_len * block_len * HEAD * 9 * pair_count * head_count
    return pl.pallas_call(
        span_kernel,
        grid_spec=pltpu.PrefetchScalarGridSpec(
            num_scalar_prefetch=1,
            grid=(head_count,),
            in_specs=[
                pl.BlockSpec((span_count, span_len, HEAD), window_map),
                pl.BlockSpec((span_count, span_len, HEAD), window_map),
                pl.BlockSpec((slot_count, 2, block_len, HEAD), block_map),
            ],
            out_specs=[
                pl.BlockSpec((span_count, span_len, HEAD), window_map),
                pl.BlockSpec((pair_count, 2, block_len, HEAD), block_map),
            ],
        ),
        out_shape=[
            jax.ShapeDtypeStruct((span_count, span_len, row_width), jnp.bfloat16),
            jax.ShapeDtypeStruct((pair_count, 2, block_len, row_width), jnp.bfloat16),
        ],
        cost_estimate=pl.CostEstimate(
            flops=flops,
            transcendentals=2 * pair_count * span_len * block_len * head_count,
            bytes_accessed=2 * (2 * blocks.size + 3 * window_query.size),
        ),
    )(pair_slot, window_query, window_grad, blocks)


def gather_kernel(key_ref, value_ref, out_ref, send_sem, recv_sem, local_sem):
    groups = lax.axis_size("grp")
    me = lax.axis_index("grp")
    column = lax.axis_index("seq")
    ahead = groups // 2
    behind = groups - 1 - ahead
    up = lax.rem(me + 1, groups)
    down = lax.rem(me + groups - 1, groups)
    barrier = pltpu.get_barrier_semaphore()
    for neighbour in (up, down):
        pl.semaphore_signal(
            barrier, 1, device_id=(neighbour, column), device_id_type=pl.DeviceIdType.MESH
        )
    pl.semaphore_wait(barrier, 2)
    own = (key_ref.at[0, 0], value_ref.at[0, 0])
    locals_ = [
        pltpu.make_async_copy(own[kind], out_ref.at[0, kind], local_sem.at[kind]) for kind in range(2)
    ]
    for copy in locals_:
        copy.start()
    for step in range(1, ahead + 1):
        routes = [(0, groups + 1 - step, groups - step, up)]
        if step <= behind:
            routes.append((1, step - 1, step, down))
        copies = []
        for direction, source, target, device in routes:
            if step == 1:
                pieces = [(own[kind], out_ref.at[target, kind], kind) for kind in range(2)]
            else:
                pieces = [(out_ref.at[source], out_ref.at[target], 0)]
            for src, dst, part in pieces:
                copies.append(
                    pltpu.make_async_remote_copy(
                        src_ref=src,
                        dst_ref=dst,
                        send_sem=send_sem.at[direction, step - 1, part],
                        recv_sem=recv_sem.at[direction, step - 1, part],
                        device_id=(device, column),
                        device_id_type=pl.DeviceIdType.MESH,
                    )
                )
        for copy in copies:
            copy.start()
        for copy in copies:
            copy.wait()
    for copy in locals_:
        copy.wait()


def ring_gather(keys, values, groups):
    ahead = groups // 2
    block_shape = keys.shape[2:]
    return pl.pallas_call(
        gather_kernel,
        out_shape=jax.ShapeDtypeStruct((groups, 2) + block_shape, keys.dtype),
        in_specs=[pl.BlockSpec(memory_space=pl.ANY), pl.BlockSpec(memory_space=pl.ANY)],
        out_specs=pl.BlockSpec(memory_space=pltpu.VMEM),
        scratch_shapes=[
            pltpu.SemaphoreType.DMA((2, ahead, 2)),
            pltpu.SemaphoreType.DMA((2, ahead, 2)),
            pltpu.SemaphoreType.DMA((2,)),
        ],
        compiler_params=pltpu.CompilerParams(
            collective_id=0, has_side_effects=True, vmem_limit_bytes=60 * 1024 * 1024
        ),
    )(keys, values)


def add_rows(target, first, second):
    rows = 16

    def body(index, carry):
        part = pl.ds(pl.multiple_of(index * rows, rows), rows)
        for kind in range(target.shape[0]):
            total = first[kind, part].astype(jnp.float32) + second[kind, part].astype(jnp.float32)
            target[kind, part] = total.astype(target.dtype)
        return carry

    lax.fori_loop(0, target.shape[1] // rows, body, 0)


def reduce_kernel(term_ref, out_ref, own, recv_up, recv_down, send_up, send_down, local_sem, send_sem, recv_sem):
    groups = lax.axis_size("grp")
    me = lax.axis_index("grp")
    column = lax.axis_index("seq")
    ahead = groups // 2
    behind = groups - 1 - ahead
    up = lax.rem(me + 1, groups)
    down = lax.rem(me + groups - 1, groups)
    barrier = pltpu.get_barrier_semaphore()
    for neighbour in (up, down):
        pl.semaphore_signal(
            barrier, 1, device_id=(neighbour, column), device_id_type=pl.DeviceIdType.MESH
        )
    pl.semaphore_wait(barrier, 2)
    load = pltpu.make_async_copy(term_ref, own, local_sem)
    load.start()
    for step in range(1, ahead + 1):
        if step == 2:
            load.wait()
        routes = [(0, up, recv_up, send_up, term_ref.at[ahead], ahead - step + 1)]
        if step <= behind:
            routes.append((1, down, recv_down, send_down, term_ref.at[groups - behind], groups - behind + step - 1))
        copies = []
        for direction, device, recv, send, first, slot in routes:
            if step == 1:
                source = first
            else:
                add_rows(send.at[step - 2], recv.at[step - 2], own.at[slot])
                source = send.at[step - 2]
            copies.append(
                pltpu.make_async_remote_copy(
                    src_ref=source,
                    dst_ref=recv.at[step - 1],
                    send_sem=send_sem.at[direction, step - 1],
                    recv_sem=recv_sem.at[direction, step - 1],
                    device_id=(device, column),
                    device_id_type=pl.DeviceIdType.MESH,
                )
            )
            copies[-1].start()
        for copy in copies:
            copy.wait()
    rows = 16

    def body(index, carry):
        part = pl.ds(pl.multiple_of(index * rows, rows), rows)
        for kind in range(out_ref.shape[0]):
            total = (
                recv_up[ahead - 1, kind, part].astype(jnp.float32)
                + recv_down[behind - 1, kind, part].astype(jnp.float32)
                + own[0, kind, part].astype(jnp.float32)
            )
            out_ref[kind, part] = total.astype(out_ref.dtype)
        return carry

    lax.fori_loop(0, out_ref.shape[1] // rows, body, 0)


def ring_reduce(terms, groups):
    ahead = groups // 2
    behind = groups - 1 - ahead
    block = terms.shape[1:]
    return pl.pallas_call(
        reduce_kernel,
        out_shape=jax.ShapeDtypeStruct(block, terms.dtype),
        in_specs=[pl.BlockSpec(memory_space=pl.ANY)],
        out_specs=pl.BlockSpec(memory_space=pltpu.VMEM),
        scratch_shapes=[
            pltpu.VMEM(terms.shape, terms.dtype),
            pltpu.VMEM((ahead,) + block, terms.dtype),
            pltpu.VMEM((behind,) + block, terms.dtype),
            pltpu.VMEM((ahead - 1,) + block, terms.dtype),
            pltpu.VMEM((behind - 1,) + block, terms.dtype),
            pltpu.SemaphoreType.DMA(()),
            pltpu.SemaphoreType.DMA((2, ahead)),
            pltpu.SemaphoreType.DMA((2, ahead)),
        ],
        compiler_params=pltpu.CompilerParams(
            collective_id=1, has_side_effects=True, vmem_limit_bytes=60 * 1024 * 1024
        ),
    )(terms)


def ring_step(array, axis, by):
    length = lax.axis_size(axis)
    pairs = [(i, (i + by) % length) for i in range(length)]
    return lax.ppermute(array, axis, pairs)


def shards(queries, grad_out, neighbour_keys, neighbour_values, neighbours):
    groups = lax.axis_size("grp")
    me = lax.axis_index("grp")
    span_len = SPAN
    tok_rows = queries.shape[1]
    row_width = queries.shape[2]
    head_count = row_width // HEAD
    neighbour_len = neighbour_keys.shape[2]
    span_count = tok_rows // span_len
    pair_count = span_count * NBRS
    assert pair_count == groups
    score_scale = HEAD ** (-0.5)
    ahead = groups // 2
    behind = groups - 1 - ahead
    next_query, next_grad = from_behind(
        (queries[0, : span_len - 1], grad_out[0, : span_len - 1]), "seq", -1
    )
    window_query = jnp.concatenate([queries[0, span_len - 1 :], next_query], axis=0).reshape(
        span_count, span_len, row_width
    )
    window_grad = jnp.concatenate([grad_out[0, span_len - 1 :], next_grad], axis=0).reshape(
        span_count, span_len, row_width
    )
    owner_ids = neighbours[0].reshape(pair_count)
    group_ids = jnp.arange(groups, dtype=jnp.int32)
    placement = (owner_ids[None, :] == group_ids[:, None]).astype(jnp.int32)
    rel_groups = (me + group_ids) % groups
    pair_slot = (owner_ids - me) % groups
    all_blocks = ring_gather(neighbour_keys, neighbour_values, groups)
    grad_windows, pair_terms = span_attention(pair_slot, window_query, window_grad, all_blocks)
    grad_windows = grad_windows.reshape(1, span_count, span_len, row_width)
    total = ring_reduce(pair_terms, groups)
    grad_keys = total[0].astype(jnp.bfloat16).reshape(1, 1, neighbour_len, row_width)
    grad_values = total[1].astype(jnp.bfloat16).reshape(1, 1, neighbour_len, row_width)
    return (grad_windows, grad_keys, grad_values)


def solution(mesh):
    in_specs = (
        P("grp", "seq", None),
        P("grp", "seq", None),
        P("grp", "seq", None, None),
        P("grp", "seq", None, None),
        P("grp", "seq", None),
    )
    out_specs = (
        P("grp", "seq", None, None),
        P("grp", "seq", None, None),
        P("grp", "seq", None, None),
    )
    return jax.shard_map(shards, mesh=mesh, in_specs=in_specs, out_specs=out_specs, check_vma=False)
```

```python
import jax
import jax.numpy as jnp
from jax import lax
from jax.experimental import pallas as pl
from jax.experimental.pallas import tpu as pltpu
from jax.sharding import PartitionSpec as P

HEAD = 128
SPAN = 64
NBRS = 4


def from_behind(array, axis, by):
    length = lax.axis_size(axis)
    pairs = [(i, i + by) for i in range(length) if 0 <= i + by < length]
    return lax.ppermute(array, axis, pairs)


def span_kernel(slot_ref, query_ref, grad_ref, block_ref, window_ref, term_ref):
    for head in range(query_ref.shape[-1] // HEAD):
        cols = pl.ds(head * HEAD, HEAD)
        head_kernel(slot_ref, query_ref, grad_ref, block_ref, window_ref, term_ref, cols)


def head_kernel(slot_ref, query_ref, grad_ref, block_ref, window_ref, term_ref, cols):
    scale = HEAD ** (-0.5)
    contract_last = (((1,), (1,)), ((), ()))
    plain = (((1,), (0,)), ((), ()))
    for span in range(query_ref.shape[0]):
        query = query_ref[span, :, cols]
        grad = grad_ref[span, :, cols]
        slots = [slot_ref[span * NBRS + j] for j in range(NBRS)]
        keys = jnp.concatenate([block_ref[slot, 0, :, cols] for slot in slots], axis=0)
        values = jnp.concatenate([block_ref[slot, 1, :, cols] for slot in slots], axis=0)
        scores = lax.dot_general(query, keys, contract_last, preferred_element_type=jnp.float32) * scale
        grad_probs = lax.dot_general(grad, values, contract_last, preferred_element_type=jnp.float32)
        maxes, totals, dots = [], [], []
        for j in range(NBRS):
            part = scores[:, j * HEAD : (j + 1) * HEAD]
            row_max = jnp.max(part, axis=-1, keepdims=True)
            exp_part = jnp.exp(part - row_max)
            row_total = jnp.sum(exp_part, axis=-1, keepdims=True)
            rounded = exp_part.astype(jnp.bfloat16).astype(jnp.float32)
            dotted = jnp.sum(
                rounded * grad_probs[:, j * HEAD : (j + 1) * HEAD], axis=-1, keepdims=True
            )
            maxes.append(row_max)
            totals.append(row_total)
            dots.append(dotted / row_total)
        top = maxes[0]
        for j in range(1, NBRS):
            top = jnp.maximum(top, maxes[j])
        weights = [totals[j] * jnp.exp(maxes[j] - top) for j in range(NBRS)]
        weight_sum = weights[0]
        weighted = weights[0] * dots[0]
        for j in range(1, NBRS):
            weight_sum = weight_sum + weights[j]
            weighted = weighted + weights[j] * dots[j]
        log_total = top + jnp.log(weight_sum)
        delta = weighted / weight_sum
        probs = jnp.exp(scores - log_total)
        grad_scores = (probs * (grad_probs - delta)).astype(jnp.bfloat16)
        window = jnp.zeros(query.shape, jnp.float32)
        for j in range(NBRS):
            part = lax.dot_general(
                grad_scores[:, j * HEAD : (j + 1) * HEAD],
                keys[j * HEAD : (j + 1) * HEAD],
                plain,
                preferred_element_type=jnp.float32,
            )
            window = window + (part * scale).astype(jnp.bfloat16).astype(jnp.float32)
        window_ref[span, :, cols] = window.astype(window_ref.dtype)
        contract_first = (((0,), (0,)), ((), ()))
        value_term = lax.dot_general(
            probs.astype(jnp.bfloat16), grad, contract_first, preferred_element_type=jnp.float32
        )
        key_term = (
            lax.dot_general(grad_scores, query, contract_first, preferred_element_type=jnp.float32)
            * scale
        )
        for j in range(NBRS):
            term_ref[slots[j], 0, :, cols] = key_term[j * HEAD : (j + 1) * HEAD].astype(term_ref.dtype)
            term_ref[slots[j], 1, :, cols] = value_term[j * HEAD : (j + 1) * HEAD].astype(term_ref.dtype)


def span_attention(pair_slot, window_query, window_grad, blocks):
    span_count, span_len, row_width = window_query.shape
    slot_count, _, block_len, _ = blocks.shape
    head_count = row_width // HEAD
    width = 2 * HEAD
    pair_count = span_count * NBRS

    def window_map(h, slots):
        return (0, 0, h)

    def block_map(h, slots):
        return (0, 0, 0, h)

    flops = 2 * span_len * block_len * HEAD * 9 * pair_count * head_count
    return pl.pallas_call(
        span_kernel,
        grid_spec=pltpu.PrefetchScalarGridSpec(
            num_scalar_prefetch=1,
            grid=(row_width // width,),
            in_specs=[
                pl.BlockSpec((span_count, span_len, width), window_map),
                pl.BlockSpec((span_count, span_len, width), window_map),
                pl.BlockSpec((slot_count, 2, block_len, width), block_map),
            ],
            out_specs=[
                pl.BlockSpec((span_count, span_len, width), window_map),
                pl.BlockSpec((pair_count, 2, block_len, width), block_map),
            ],
        ),
        out_shape=[
            jax.ShapeDtypeStruct((span_count, span_len, row_width), jnp.bfloat16),
            jax.ShapeDtypeStruct((pair_count, 2, block_len, row_width), jnp.bfloat16),
        ],
        cost_estimate=pl.CostEstimate(
            flops=flops,
            transcendentals=2 * pair_count * span_len * block_len * head_count,
            bytes_accessed=2 * (2 * blocks.size + 3 * window_query.size),
        ),
    )(pair_slot, window_query, window_grad, blocks)


def gather_kernel(key_ref, value_ref, out_ref, send_sem, recv_sem, local_sem):
    groups = lax.axis_size("grp")
    me = lax.axis_index("grp")
    column = lax.axis_index("seq")
    ahead = groups // 2
    behind = groups - 1 - ahead
    up = lax.rem(me + 1, groups)
    down = lax.rem(me + groups - 1, groups)
    barrier = pltpu.get_barrier_semaphore()
    for neighbour in (up, down):
        pl.semaphore_signal(
            barrier, 1, device_id=(neighbour, column), device_id_type=pl.DeviceIdType.MESH
        )
    pl.semaphore_wait(barrier, 2)
    own = (key_ref.at[0, 0], value_ref.at[0, 0])
    locals_ = [
        pltpu.make_async_copy(own[kind], out_ref.at[0, kind], local_sem.at[kind]) for kind in range(2)
    ]
    for copy in locals_:
        copy.start()
    for step in range(1, ahead + 1):
        routes = [(0, groups + 1 - step, groups - step, up)]
        if step <= behind:
            routes.append((1, step - 1, step, down))
        copies = []
        for direction, source, target, device in routes:
            if step == 1:
                pieces = [(own[kind], out_ref.at[target, kind], kind) for kind in range(2)]
            else:
                pieces = [(out_ref.at[source], out_ref.at[target], 0)]
            for src, dst, part in pieces:
                copies.append(
                    pltpu.make_async_remote_copy(
                        src_ref=src,
                        dst_ref=dst,
                        send_sem=send_sem.at[direction, step - 1, part],
                        recv_sem=recv_sem.at[direction, step - 1, part],
                        device_id=(device, column),
                        device_id_type=pl.DeviceIdType.MESH,
                    )
                )
        for copy in copies:
            copy.start()
        for copy in copies:
            copy.wait()
    for copy in locals_:
        copy.wait()


def ring_gather(keys, values, groups):
    ahead = groups // 2
    block_shape = keys.shape[2:]
    return pl.pallas_call(
        gather_kernel,
        out_shape=jax.ShapeDtypeStruct((groups, 2) + block_shape, keys.dtype),
        in_specs=[pl.BlockSpec(memory_space=pl.ANY), pl.BlockSpec(memory_space=pl.ANY)],
        out_specs=pl.BlockSpec(memory_space=pl.ANY),
        scratch_shapes=[
            pltpu.SemaphoreType.DMA((2, ahead, 2)),
            pltpu.SemaphoreType.DMA((2, ahead, 2)),
            pltpu.SemaphoreType.DMA((2,)),
        ],
        compiler_params=pltpu.CompilerParams(collective_id=0, has_side_effects=True),
    )(keys, values)


def add_rows(target, first, second):
    rows = 16

    def body(index, carry):
        part = pl.ds(pl.multiple_of(index * rows, rows), rows)
        for kind in range(target.shape[0]):
            total = first[kind, part].astype(jnp.float32) + second[kind, part].astype(jnp.float32)
            target[kind, part] = total.astype(target.dtype)
        return carry

    lax.fori_loop(0, target.shape[1] // rows, body, 0)


def reduce_kernel(term_ref, out_ref, own, recv_up, recv_down, send_up, send_down, local_sem, send_sem, recv_sem):
    groups = lax.axis_size("grp")
    me = lax.axis_index("grp")
    column = lax.axis_index("seq")
    ahead = groups // 2
    behind = groups - 1 - ahead
    up = lax.rem(me + 1, groups)
    down = lax.rem(me + groups - 1, groups)
    barrier = pltpu.get_barrier_semaphore()
    for neighbour in (up, down):
        pl.semaphore_signal(
            barrier, 1, device_id=(neighbour, column), device_id_type=pl.DeviceIdType.MESH
        )
    pl.semaphore_wait(barrier, 2)
    load = pltpu.make_async_copy(term_ref, own, local_sem)
    load.start()
    for step in range(1, ahead + 1):
        if step == 2:
            load.wait()
        routes = [(0, up, recv_up, send_up, term_ref.at[ahead], ahead - step + 1)]
        if step <= behind:
            routes.append((1, down, recv_down, send_down, term_ref.at[groups - behind], groups - behind + step - 1))
        copies = []
        for direction, device, recv, send, first, slot in routes:
            if step == 1:
                source = first
            else:
                add_rows(send.at[step - 2], recv.at[step - 2], own.at[slot])
                source = send.at[step - 2]
            copies.append(
                pltpu.make_async_remote_copy(
                    src_ref=source,
                    dst_ref=recv.at[step - 1],
                    send_sem=send_sem.at[direction, step - 1],
                    recv_sem=recv_sem.at[direction, step - 1],
                    device_id=(device, column),
                    device_id_type=pl.DeviceIdType.MESH,
                )
            )
            copies[-1].start()
        for copy in copies:
            copy.wait()
    rows = 16

    def body(index, carry):
        part = pl.ds(pl.multiple_of(index * rows, rows), rows)
        for kind in range(out_ref.shape[0]):
            total = (
                recv_up[ahead - 1, kind, part].astype(jnp.float32)
                + recv_down[behind - 1, kind, part].astype(jnp.float32)
                + own[0, kind, part].astype(jnp.float32)
            )
            out_ref[kind, part] = total.astype(out_ref.dtype)
        return carry

    lax.fori_loop(0, out_ref.shape[1] // rows, body, 0)


def ring_reduce(terms, groups):
    ahead = groups // 2
    behind = groups - 1 - ahead
    block = terms.shape[1:]
    return pl.pallas_call(
        reduce_kernel,
        out_shape=jax.ShapeDtypeStruct(block, terms.dtype),
        in_specs=[pl.BlockSpec(memory_space=pl.ANY)],
        out_specs=pl.BlockSpec(memory_space=pltpu.VMEM),
        scratch_shapes=[
            pltpu.VMEM(terms.shape, terms.dtype),
            pltpu.VMEM((ahead,) + block, terms.dtype),
            pltpu.VMEM((behind,) + block, terms.dtype),
            pltpu.VMEM((ahead - 1,) + block, terms.dtype),
            pltpu.VMEM((behind - 1,) + block, terms.dtype),
            pltpu.SemaphoreType.DMA(()),
            pltpu.SemaphoreType.DMA((2, ahead)),
            pltpu.SemaphoreType.DMA((2, ahead)),
        ],
        compiler_params=pltpu.CompilerParams(
            collective_id=1, has_side_effects=True, vmem_limit_bytes=60 * 1024 * 1024
        ),
    )(terms)


def ring_step(array, axis, by):
    length = lax.axis_size(axis)
    pairs = [(i, (i + by) % length) for i in range(length)]
    return lax.ppermute(array, axis, pairs)


def shards(queries, grad_out, neighbour_keys, neighbour_values, neighbours):
    groups = lax.axis_size("grp")
    me = lax.axis_index("grp")
    span_len = SPAN
    tok_rows = queries.shape[1]
    row_width = queries.shape[2]
    head_count = row_width // HEAD
    neighbour_len = neighbour_keys.shape[2]
    span_count = tok_rows // span_len
    pair_count = span_count * NBRS
    assert pair_count == groups
    score_scale = HEAD ** (-0.5)
    ahead = groups // 2
    behind = groups - 1 - ahead
    next_query, next_grad = from_behind(
        (queries[0, : span_len - 1], grad_out[0, : span_len - 1]), "seq", -1
    )
    window_query = jnp.concatenate([queries[0, span_len - 1 :], next_query], axis=0).reshape(
        span_count, span_len, row_width
    )
    window_grad = jnp.concatenate([grad_out[0, span_len - 1 :], next_grad], axis=0).reshape(
        span_count, span_len, row_width
    )
    owner_ids = neighbours[0].reshape(pair_count)
    group_ids = jnp.arange(groups, dtype=jnp.int32)
    placement = (owner_ids[None, :] == group_ids[:, None]).astype(jnp.int32)
    rel_groups = (me + group_ids) % groups
    pair_slot = (owner_ids - me) % groups
    all_blocks = ring_gather(neighbour_keys, neighbour_values, groups)
    grad_windows, pair_terms = span_attention(pair_slot, window_query, window_grad, all_blocks)
    grad_windows = grad_windows.reshape(1, span_count, span_len, row_width)
    total = ring_reduce(pair_terms, groups)
    grad_keys = total[0].astype(jnp.bfloat16).reshape(1, 1, neighbour_len, row_width)
    grad_values = total[1].astype(jnp.bfloat16).reshape(1, 1, neighbour_len, row_width)
    return (grad_windows, grad_keys, grad_values)


def solution(mesh):
    in_specs = (
        P("grp", "seq", None),
        P("grp", "seq", None),
        P("grp", "seq", None, None),
        P("grp", "seq", None, None),
        P("grp", "seq", None),
    )
    out_specs = (
        P("grp", "seq", None, None),
        P("grp", "seq", None, None),
        P("grp", "seq", None, None),
    )
    return jax.shard_map(shards, mesh=mesh, in_specs=in_specs, out_specs=out_specs, check_vma=False)
```
